128 devices in a mesh: gx: 16 (over x, z), gy: 8 (over y, core).
Axes of the slice: x: 4, y: 4, z: 4, core: 2. Of those that a mesh axis runs over, the one named last changes fastest.
Arguments:
- factor_grads: bfloat16 [512, 196608], P(('gx', 'gy')), may hold values from -0.29882812 to 0.29882812
- latents: bfloat16 [512, 1024], P(('gx', 'gy')), may hold values from -6 to 6
- task_ids: int32 [512], P(('gx', 'gy')), may hold values from 0 to 511, each once
- offsets: int32 [160], replicated, may hold values from 0 to 196607, as said below
- target_scale: float32 [160], replicated, may hold values from 0.5 to 2
- momentum: float32 [1024, 196608], P(None, ('gx', 'gy')), may hold values from -6 to 6
Outputs:
- new_momentum: float32 [1024, 196608], P(None, ('gx', 'gy'))
- step: float32 [1024, 196608], P(None, ('gx', 'gy'))
The draws below stay inside these ranges and needn't reach their ends.
Inputs may be any that keep to these rules, and one draw needn't show every extreme that they name: `task_ids`: a permutation of 0 to 511. offsets[0] is 0 and offsets rise strictly.
All inputs are finite; a program needn't handle non-finite values.
Results may differ from the reference program's by a relative error of at most 0.0003.
Values may be sent and summed in bfloat16 or wider, within the bound.
A program may use at most 128 MiB of HBM per device.

```python
import math
import jax
import jax.numpy as jnp
from jax import lax

L = 1024
OUT = 196608
TARGETS = 160
ITERS = 2
TASKS = 512


def draw_offsets(key, part):
    cut_points = jax.random.permutation(key, OUT - 1)[:TARGETS - 1] + 1
    cut_points = jnp.sort(cut_points.astype(jnp.int32))
    return jnp.concatenate([jnp.zeros((1,), jnp.int32), cut_points]).astype(jnp.int32)


def block_levels(key, dims, shards, low, high):
    def one(axis_at, blocks):
        draws = jax.random.uniform(jax.random.fold_in(jax.random.fold_in(key, 6), axis_at), (blocks,), jnp.float32, low / len(shards), high / len(shards))
        return jnp.repeat(jnp.exp(draws), dims[axis_at] // blocks).reshape((-1,) + (1,) * (len(dims) - axis_at - 1))

    factor_of = one(*shards[0])
    for cut in shards[1:]:
        factor_of = factor_of * one(*cut)
    return factor_of


def gaussian(stream_key, shape, spread, limit, cuts=(), kind=jnp.bfloat16):
    entries = jax.random.normal(stream_key, shape, jnp.float32) * spread
    if len(cuts) > 0:
        entries = block_levels(stream_key, shape, cuts, -0.22, 0.18) * entries
    return jnp.clip(entries, min=-limit, max=limit).astype(kind)


def setup_inputs(seed: int = 0) -> dict:
    key_list = jax.random.split(jax.random.key(seed), 7)
    return {
        "factor_grads": gaussian(key_list[0], (TASKS, OUT), 0.05, 0.29882812, ((0, 128),)),
        "latents": gaussian(key_list[1], (TASKS, L), 1.0, 6.0, ((0, 128),)),
        "task_ids": jax.random.permutation(key_list[2], TASKS).astype(jnp.int32),
        "offsets": draw_offsets(jax.random.fold_in(key_list[6], 71), 0),
        "target_scale": jnp.clip(jnp.exp(jax.random.uniform(key_list[4], (TARGETS,), jnp.float32, math.log(0.5), math.log(2.0))), 0.5, 2.0),
        "momentum": gaussian(key_list[5], (L, OUT), 1.0, 6.0, ((1, 128),), jnp.float32),
    }


MOMENTUM_DECAY = 0.95
EPSILON = 1e-07
NEWTON_A = 3.4445
NEWTON_B = -4.775
NEWTON_C = 2.0315

def reference(factor_grads, latents, task_ids, offsets, target_scale, momentum):
    task_latent = latents[task_ids]
    head_grad = jnp.dot(task_latent.T, factor_grads, preferred_element_type=jnp.float32)
    new_momentum = MOMENTUM_DECAY * momentum + head_grad
    blended = head_grad + MOMENTUM_DECAY * new_momentum
    frobenius = jnp.sqrt(jnp.sum(blended * blended))
    orthogonal = blended / (frobenius + EPSILON)
    for iteration in range(ITERS):
        gram_matrix = jnp.dot(orthogonal, orthogonal.T, precision=lax.Precision.HIGHEST)
        poly_matrix = NEWTON_B * gram_matrix + NEWTON_C * jnp.dot(gram_matrix, gram_matrix, precision=lax.Precision.HIGHEST)
        orthogonal = NEWTON_A * orthogonal + jnp.dot(poly_matrix, orthogonal, precision=lax.Precision.HIGHEST)
    column_index = jnp.arange(OUT, dtype=jnp.int32)
    target_index = (jnp.searchsorted(offsets, column_index, side='right') - 1).astype(jnp.int32)
    column_scale = target_scale[target_index]
    step = math.sqrt(OUT) * column_scale[None, :] * orthogonal
    return (new_momentum, step)
```

```python
import functools
import math

import jax
import jax.numpy as jnp
from jax import lax
from jax.experimental import pallas as pl
from jax.experimental.pallas import tpu as pltpu
from jax.sharding import PartitionSpec as P

OUT = 196608
MOMENTUM_DECAY = 0.95
EPSILON = 1e-07
NEWTON_A = 3.4445
NEWTON_B = -4.775
NEWTON_C = 2.0315

BLOCK = 256
NBLK = 4
NPAIR = 10
CHUNK = 512
F32 = jnp.float32
BF16 = jnp.bfloat16


def split(value):
    high = value.astype(BF16)
    return high, (value - high.astype(F32)).astype(BF16)


def mxu(left, right):
    return lax.dot_general(left, right, (((1,), (0,)), ((), ())), preferred_element_type=F32)


def mxu_t(left, right):
    return lax.dot_general(left, right, (((1,), (1,)), ((), ())), preferred_element_type=F32)


def pair_of(slot):
    row = lax.rem(slot, NBLK)
    col = lax.rem(row + lax.div(slot, NBLK), NBLK)
    return row, col


def front_kernel(lat_ref, cols_ref, mom_ref, newmom_ref, high_ref, low_ref, gram_ref, tlt_ref):
    step = pl.program_id(0)
    tasks = lat_ref.shape[0]
    width = tlt_ref.shape[0]

    @pl.when(step == 0)
    def _():
        tail = lat_ref[:, width:].astype(F32)
        ids = jnp.sum(tail, axis=1, keepdims=True)
        which = lax.broadcasted_iota(jnp.int32, (tasks, tasks), 1).astype(F32)
        onehot = jnp.where(which == ids, 1.0, 0.0).astype(BF16)
        task_latent = mxu(onehot, lat_ref[:, :width])
        tlt_ref[...] = task_latent.T.astype(BF16)
        gram_ref[...] = jnp.zeros_like(gram_ref)

    for i in range(NBLK):
        rows = slice(i * BLOCK, (i + 1) * BLOCK)
        head = mxu(tlt_ref[rows, :], cols_ref[...])
        new_momentum = MOMENTUM_DECAY * mom_ref[rows, :] + head
        newmom_ref[rows, :] = new_momentum
        high, low = split(head + MOMENTUM_DECAY * new_momentum)
        high_ref[rows, :] = high
        low_ref[rows, :] = low

    def body(slot, carry):
        row, col = pair_of(slot)
        rows = pl.ds(pl.multiple_of(row * BLOCK, BLOCK), BLOCK)
        cols = pl.ds(pl.multiple_of(col * BLOCK, BLOCK), BLOCK)
        gram_ref[slot] += (
            mxu_t(high_ref[rows, :], high_ref[cols, :])
            + mxu_t(high_ref[rows, :], low_ref[cols, :])
            + mxu_t(low_ref[rows, :], high_ref[cols, :])
        )
        return carry

    lax.fori_loop(0, NPAIR, body, 0)


def front(lat, cols, momentum):
    width, count = momentum.shape
    tasks = lat.shape[0]
    grid = count // CHUNK
    return pl.pallas_call(
        front_kernel,
        grid=(grid,),
        in_specs=[
            pl.BlockSpec(lat.shape, lambda c: (0, 0)),
            pl.BlockSpec((tasks, CHUNK), lambda c: (0, c)),
            pl.BlockSpec((width, CHUNK), lambda c: (0, c)),
        ],
        out_specs=[
            pl.BlockSpec((width, CHUNK), lambda c: (0, c)),
            pl.BlockSpec((width, CHUNK), lambda c: (0, c)),
            pl.BlockSpec((width, CHUNK), lambda c: (0, c)),
            pl.BlockSpec((NPAIR, BLOCK, BLOCK), lambda c: (0, 0, 0)),
        ],
        out_shape=[
            jax.ShapeDtypeStruct((width, count), F32),
            jax.ShapeDtypeStruct((width, count), BF16),
            jax.ShapeDtypeStruct((width, count), BF16),
            jax.ShapeDtypeStruct((NPAIR, BLOCK, BLOCK), F32),
        ],
        scratch_shapes=[pltpu.VMEM((width, tasks), BF16)],
        compiler_params=pltpu.CompilerParams(vmem_limit_bytes=60 << 20),
        name="front",
    )(lat, cols, momentum)


def back_kernel(gram_ref, high_ref, low_ref, scale_ref, step_ref, inv_ref, mats_ref):
    G, M1, T, G2 = 0, 1, 2, 3

    def store(which, row, col, value):
        high, low = split(value)
        rows = pl.ds(pl.multiple_of(row * BLOCK, BLOCK), BLOCK)
        cols = pl.ds(pl.multiple_of(col * BLOCK, BLOCK), BLOCK)
        mats_ref[which, 0, col, rows, :] = high
        mats_ref[which, 1, col, rows, :] = low
        flipped, flipped_low = split(value.T)
        mats_ref[which, 0, row, cols, :] = flipped
        mats_ref[which, 1, row, cols, :] = flipped_low

    def eye(row, col):
        r = lax.broadcasted_iota(jnp.int32, (BLOCK, BLOCK), 0)
        c = lax.broadcasted_iota(jnp.int32, (BLOCK, BLOCK), 1)
        return jnp.where((r == c) & (row == col), 1.0, 0.0)

    def product(left, right, row, col):
        rows = pl.ds(pl.multiple_of(row * BLOCK, BLOCK), BLOCK)
        total = None
        for k in range(NBLK):
            ks = slice(k * BLOCK, (k + 1) * BLOCK)
            lh, ll = mats_ref[left, 0, k, rows, :], mats_ref[left, 1, k, rows, :]
            rh, rl = mats_ref[right, 0, col, ks, :], mats_ref[right, 1, col, ks, :]
            term = mxu(lh, rh) + mxu(lh, rl) + mxu(ll, rh)
            total = term if total is None else total + term
        return total

    def stage(left, right, dest, finish):
        def body(slot, carry):
            row, col = pair_of(slot)
            store(dest, row, col, finish(slot, row, col, product(left, right, row, col)))
            return carry

        lax.fori_loop(0, NPAIR, body, 0)

    @pl.when(pl.program_id(0) == 0)
    def _():
        r = lax.broadcasted_iota(jnp.int32, (BLOCK, BLOCK), 0)
        c = lax.broadcasted_iota(jnp.int32, (BLOCK, BLOCK), 1)
        diagonal = gram_ref[0] + gram_ref[1] + gram_ref[2] + gram_ref[3]
        picked = jnp.where(r == c, diagonal, 0.0)
        squares = jnp.sum(jnp.sum(picked, axis=1, keepdims=True), axis=0, keepdims=True)
        inverse = 1.0 / (jnp.sqrt(squares) + EPSILON)
        inv_ref[...] = jnp.broadcast_to(inverse, inv_ref.shape)

        def normalise(slot, carry):
            row, col = pair_of(slot)
            inv = inv_ref[0:1, 0:1]
            store(G, row, col, (gram_ref[slot] * inv) * inv)
            return carry

        lax.fori_loop(0, NPAIR, normalise, 0)

        def first(slot, row, col, value):
            inv = inv_ref[0:1, 0:1]
            return NEWTON_A * eye(row, col) + NEWTON_B * ((gram_ref[slot] * inv) * inv) + NEWTON_C * value

        def second(slot, row, col, value):
            rows = pl.ds(pl.multiple_of(row * BLOCK, BLOCK), BLOCK)
            own = mats_ref[G2, 0, col, rows, :].astype(F32) + mats_ref[G2, 1, col, rows, :].astype(F32)
            return NEWTON_A * eye(row, col) + NEWTON_B * own + NEWTON_C * value

        plain = lambda slot, row, col, value: value
        stage(G, G, M1, first)
        stage(G, M1, T, plain)
        stage(T, M1, G2, plain)
        stage(G2, G2, G, second)
        stage(G, M1, T, plain)

    factor = scale_ref[...] * (math.sqrt(OUT) * inv_ref[0:1, 0:1])
    for i in range(NBLK):
        rows = slice(i * BLOCK, (i + 1) * BLOCK)
        total = None
        for k in range(NBLK):
            ks = slice(k * BLOCK, (k + 1) * BLOCK)
            mh, ml = mats_ref[T, 0, k, rows, :], mats_ref[T, 1, k, rows, :]
            term = mxu(mh, high_ref[ks, :]) + mxu(mh, low_ref[ks, :]) + mxu(ml, high_ref[ks, :])
            total = term if total is None else total + term
        step_ref[rows, :] = total * factor


def back(gram, high, low, scale):
    width, count = high.shape
    return pl.pallas_call(
        back_kernel,
        grid=(count // CHUNK,),
        in_specs=[
            pl.BlockSpec(gram.shape, lambda c: (0, 0, 0)),
            pl.BlockSpec((width, CHUNK), lambda c: (0, c)),
            pl.BlockSpec((width, CHUNK), lambda c: (0, c)),
            pl.BlockSpec((1, CHUNK), lambda c: (0, c)),
        ],
        out_specs=pl.BlockSpec((width, CHUNK), lambda c: (0, c)),
        out_shape=jax.ShapeDtypeStruct((width, count), F32),
        scratch_shapes=[
            pltpu.VMEM((8, 128), F32),
            pltpu.VMEM((4, 2, NBLK, width, BLOCK), BF16),
        ],
        compiler_params=pltpu.CompilerParams(vmem_limit_bytes=60 << 20),
        name="back",
    )(gram, high, low, scale)


def per_device(factor_grads, latents, task_ids, offsets, target_scale, momentum):
    axes = ("gx", "gy")
    rows = latents.shape[0]
    low_part = task_ids % 16
    tail = jnp.stack([task_ids - low_part, low_part], axis=1).astype(BF16)
    tail = jnp.pad(tail, ((0, 0), (0, 126)))
    lat = lax.all_gather(jnp.concatenate([latents, tail], axis=1), axes, axis=0, tiled=True)
    columns = lax.all_to_all(factor_grads, axes, split_axis=1, concat_axis=0, tiled=True)
    new_momentum, high, low, gram = front(lat, columns, momentum)
    count = momentum.shape[1]
    column_index = lax.axis_index(axes) * count + jnp.arange(count, dtype=jnp.int32)
    following = jnp.concatenate([offsets[1:], jnp.full((1,), OUT, jnp.int32)])
    inside = (column_index[None, :] >= offsets[:, None]) & (column_index[None, :] < following[:, None])
    column_scale = jnp.sum(jnp.where(inside, target_scale[:, None], 0.0), axis=0)[None, :]
    gram = lax.psum(gram, axes)
    return new_momentum, back(gram, high, low, column_scale)


def solution(mesh):
    placed = (
        P(("gx", "gy"), None),
        P(("gx", "gy"), None),
        P(("gx", "gy")),
        P(),
        P(),
        P(None, ("gx", "gy")),
    )
    return jax.shard_map(
        per_device,
        mesh=mesh,
        in_specs=placed,
        out_specs=(P(None, ("gx", "gy")), P(None, ("gx", "gy"))),
        check_vma=False,
    )
```

```python
import math

import jax
import jax.numpy as jnp
from jax import lax
from jax.experimental import pallas as pl
from jax.experimental.pallas import tpu as pltpu
from jax.sharding import PartitionSpec as P

OUT = 196608
MOMENTUM_DECAY = 0.95
EPSILON = 1e-07
NEWTON_A = 3.4445
NEWTON_B = -4.775
NEWTON_C = 2.0315

BLOCK = 256
NBLK = 4
NPAIR = 10
CHUNK = 512
PACKED = 36 * 128
F32 = jnp.float32
BF16 = jnp.bfloat16
MESH = pl.DeviceIdType.MESH


def place():
    gx = lax.axis_index("gx")
    gy = lax.axis_index("gy")
    return lax.div(gx, 4), lax.rem(gx, 4), lax.div(gy, 2), lax.rem(gy, 2)


def peer_of(where, axis, hop):
    x, z, y, core = where
    if axis == 0:
        x = lax.rem(x + hop, 4)
    elif axis == 1:
        y = lax.rem(y + hop, 4)
    elif axis == 2:
        z = lax.rem(z + hop, 4)
    else:
        core = 1 - core
    return (x * 4 + z, y * 2 + core)


PIECE = 48


def reduce_kernel(in_ref, out_ref, half_ref, from_core, got1, sum1, got2, sum2, got3,
                  cs, cr, s1, r1, s2, r2, s3, r3, s4, r4, s5, r5, s6, r6):
    where = place()
    x, z, y, core = where
    coord = (x, y, z)
    barrier = pltpu.get_barrier_semaphore()
    partners = [peer_of(where, 3, 1)] + [peer_of(where, a, k) for a in range(3) for k in (1, 2, 3)]
    for p in partners:
        pl.semaphore_signal(barrier, inc=1, device_id=p, device_id_type=MESH)
    pl.semaphore_wait(barrier, len(partners))

    def remote(src, dst, ssem, rsem, dev):
        return pltpu.make_async_remote_copy(src_ref=src, dst_ref=dst, send_sem=ssem, recv_sem=rsem,
                                            device_id=dev, device_id_type=MESH)

    other = 1 - core
    started = []
    first = []
    for r in range(3):
        c = remote(in_ref.at[r, other], from_core.at[r], cs.at[r], cr.at[r], peer_of(where, 3, 1))
        c.start()
        first.append(c)
        started.append(c)
    hops = (2, 1, 3)
    phase = []
    for r in range(3):
        first[r].wait_recv()
        half_ref[r] = in_ref[r, core] + from_core[r]
        mine = []
        for k in hops:
            to = lax.rem(coord[r] + k, 4)
            c = remote(half_ref.at[r, to], got1.at[r, k - 1], s1.at[r, k - 1], r1.at[r, k - 1], peer_of(where, r, k))
            c.start()
            mine.append(c)
        phase.append(mine)
        started += mine
    phase2 = []
    for r in range(3):
        b = (r + 1) % 3
        for c in phase[r]:
            c.wait_recv()
        sum1[r] = (half_ref[r, coord[r]] + got1[r, 0]) + (got1[r, 1] + got1[r, 2])
        mine = []
        for k in hops:
            to = lax.rem(coord[b] + k, 4)
            c = remote(sum1.at[r, to], got2.at[r, k - 1], s2.at[r, k - 1], r2.at[r, k - 1], peer_of(where, b, k))
            c.start()
            mine.append(c)
        phase2.append(mine)
        started += mine
    phase3 = []
    for r in range(3):
        b, d = (r + 1) % 3, (r + 2) % 3
        for c in phase2[r]:
            c.wait_recv()
        sum2[r] = (sum1[r, coord[b]] + got2[r, 0]) + (got2[r, 1] + got2[r, 2])
        mine = []
        for k in hops:
            c = remote(sum2.at[r], got3.at[r, k - 1], s3.at[r, k - 1], r3.at[r, k - 1], peer_of(where, d, k))
            c.start()
            mine.append(c)
        phase3.append(mine)
        started += mine
    phase4 = []
    for r in range(3):
        b = (r + 1) % 3
        for c in phase3[r]:
            c.wait_recv()
        out_ref[r, core, coord[r], coord[b]] = (sum2[r] + got3[r, 0]) + (got3[r, 1] + got3[r, 2])
        own = out_ref.at[r, core, coord[r], coord[b]]
        mine = []
        for k in hops:
            c = remote(own, own, s4.at[r, k - 1], r4.at[r, k - 1], peer_of(where, b, k))
            c.start()
            mine.append(c)
        phase4.append(mine)
        started += mine
    phase5 = []
    for r in range(3):
        for c in phase4[r]:
            c.wait_recv()
        own = out_ref.at[r, core, coord[r]]
        mine = []
        for k in hops:
            c = remote(own, own, s5.at[r, k - 1], r5.at[r, k - 1], peer_of(where, r, k))
            c.start()
            mine.append(c)
        phase5.append(mine)
        started += mine
    last = []
    for r in range(3):
        for c in phase5[r]:
            c.wait_recv()
        own = out_ref.at[r, core]
        c = remote(own, own, s6.at[r], r6.at[r], peer_of(where, 3, 1))
        c.start()
        last.append(c)
        started.append(c)
    for c in last:
        c.wait_recv()
    for c in started:
        c.wait_send()


def reduce_gram(gram):
    shape = (3, 2, 4, 4, PIECE, 128)
    dma = pltpu.SemaphoreType.DMA
    out = pl.pallas_call(
        reduce_kernel,
        in_specs=[pl.BlockSpec(memory_space=pltpu.VMEM)],
        out_specs=pl.BlockSpec(memory_space=pltpu.VMEM),
        out_shape=jax.ShapeDtypeStruct(shape, F32),
        scratch_shapes=[
            pltpu.VMEM((3, 4, 4, PIECE, 128), F32),
            pltpu.VMEM((3, 4, 4, PIECE, 128), F32),
            pltpu.VMEM((3, 3, 4, PIECE, 128), F32),
            pltpu.VMEM((3, 4, PIECE, 128), F32),
            pltpu.VMEM((3, 3, PIECE, 128), F32),
            pltpu.VMEM((3, PIECE, 128), F32),
            pltpu.VMEM((3, 3, PIECE, 128), F32),
            dma((3,)), dma((3,)),
        ] + [dma((3, 3))] * 10 + [dma((3,)), dma((3,))],
        compiler_params=pltpu.CompilerParams(collective_id=1, has_side_effects=True),
        name="reduce_gram",
    )(gram.reshape(shape))
    return out.reshape(gram.shape)


def exchange_kernel(grads_ref, lat_ref, ids_ref, offsets_ref, scales_ref,
                    cols_ref, lats_ref, scale_ref, own_ref,
                    gs, gr, own_sem, s1, r1, s2, r2, s3, r3, s4, r4):
    where = place()
    x, z, y, core = where
    count = cols_ref.shape[2]
    total = cols_ref.shape[0]
    rows, width = lat_ref.shape
    me = lax.axis_index("gx") * 8 + lax.axis_index("gy")
    barrier = pltpu.get_barrier_semaphore()

    def device(to):
        return (lax.div(to, 8), lax.rem(to, 8))

    def greet(k, carry):
        pl.semaphore_signal(barrier, inc=1, device_id=device(lax.rem(me + k, total)), device_id_type=MESH)
        return carry

    lax.fori_loop(1, total, greet, 0)

    own_ref[:, :width] = lat_ref[...]
    at_row = lax.broadcasted_iota(jnp.int32, (rows, 128), 0)
    at_lane = lax.broadcasted_iota(jnp.int32, (rows, 128), 1)
    ids = jnp.zeros((rows, 128), jnp.int32)
    for r in range(rows):
        ids = jnp.where(at_row == r, ids_ref[r], ids)
    fine = jnp.bitwise_and(ids, 15)
    tail = jnp.where(at_lane == 0, ids - fine, jnp.where(at_lane == 1, fine, 0))
    own_ref[:, width:] = tail.astype(F32).astype(BF16)

    column = me * count + 128 * lax.broadcasted_iota(jnp.int32, scale_ref.shape, 0)
    column = column + lax.broadcasted_iota(jnp.int32, scale_ref.shape, 1)

    def level(t, value):
        return jnp.where(column >= offsets_ref[t], scales_ref[t], value)

    scale_ref[...] = lax.fori_loop(0, offsets_ref.shape[0], level, jnp.zeros(scale_ref.shape, F32))

    pl.semaphore_wait(barrier, total - 1)

    def remote(src, dst, ssem, rsem, dev):
        copy = pltpu.make_async_remote_copy(
            src_ref=src, dst_ref=dst, send_sem=ssem, recv_sem=rsem, device_id=dev, device_id_type=MESH)
        copy.start()
        return copy

    keep = pltpu.make_async_copy(own_ref, lats_ref.at[x, z, y, core], own_sem)
    keep.start()
    started = []
    first = [remote(own_ref, lats_ref.at[x, z, y, core], s1.at[k - 1], r1.at[k - 1], peer_of(where, 1, k))
             for k in (2, 1, 3)]
    own = pltpu.make_async_copy(
        grads_ref.at[:, pl.ds(pl.multiple_of(me * count, count), count)], cols_ref.at[me], gr)
    own.start()

    def send(k, carry):
        to = lax.rem(me + lax.rem(k * 37, total), total)
        pltpu.make_async_remote_copy(
            src_ref=grads_ref.at[:, pl.ds(pl.multiple_of(to * count, count), count)],
            dst_ref=cols_ref.at[me], send_sem=gs, recv_sem=gr,
            device_id=device(to), device_id_type=MESH).start()
        return carry

    lax.fori_loop(1, 24, send, 0)
    keep.wait()
    for copy in first:
        copy.wait_recv()
    part = lats_ref.at[x, z, :, core]
    second = [remote(part, part, s2.at[k - 1], r2.at[k - 1], peer_of(where, 2, k)) for k in (2, 1, 3)]
    lax.fori_loop(24, 56, send, 0)
    for copy in second:
        copy.wait_recv()
    part = lats_ref.at[x, :, :, core]
    third = [remote(part, part, s3.at[k - 1], r3.at[k - 1], peer_of(where, 0, k)) for k in (2, 1, 3)]
    lax.fori_loop(56, total, send, 0)
    for copy in third:
        copy.wait_recv()
    part = lats_ref.at[:, :, :, core]
    last = remote(part, part, s4, r4, peer_of(where, 3, 1))
    last.wait_recv()
    pltpu.make_async_copy(cols_ref, cols_ref, gr).wait()
    rest = cols_ref.at[pl.ds(0, total - 1)]
    pltpu.make_async_copy(rest, rest, gs).wait()
    for copy in first + second + third + [last]:
        copy.wait_send()


def exchange(grads, lat, ids, offsets, scales):
    total = 128
    rows, width = lat.shape
    count = grads.shape[1] // total
    dma = pltpu.SemaphoreType.DMA
    smem = pl.BlockSpec(memory_space=pltpu.SMEM)
    vmem = pl.BlockSpec(memory_space=pltpu.VMEM)
    anywhere = pl.BlockSpec(memory_space=pl.ANY)
    return pl.pallas_call(
        exchange_kernel,
        in_specs=[anywhere, vmem, smem, smem, smem],
        out_specs=[anywhere, vmem, vmem],
        out_shape=[
            jax.ShapeDtypeStruct((total, rows, count), grads.dtype),
            jax.ShapeDtypeStruct((4, 4, 4, 2, rows, width + 128), lat.dtype),
            jax.ShapeDtypeStruct((count // 128, 128), F32),
        ],
        scratch_shapes=[pltpu.VMEM((rows, width + 128), lat.dtype), dma, dma, dma]
        + [dma((3,))] * 6 + [dma, dma],
        compiler_params=pltpu.CompilerParams(collective_id=2, has_side_effects=True),
        name="exchange",
    )(grads, lat, ids, offsets, scales)


def split(value):
    high = value.astype(BF16)
    return high, (value - high.astype(F32)).astype(BF16)


def mxu(left, right):
    return lax.dot_general(left, right, (((1,), (0,)), ((), ())), preferred_element_type=F32)


def mxu_t(left, right):
    return lax.dot_general(left, right, (((1,), (1,)), ((), ())), preferred_element_type=F32)


def pair_of(slot):
    row = lax.rem(slot, NBLK)
    col = lax.rem(row + lax.div(slot, NBLK), NBLK)
    return row, col


def quarters(slot):
    return ((0, 0), (0, 1), (1, 1)) if slot < NBLK else ((0, 0), (0, 1), (1, 0), (1, 1))


def first_of(slot):
    return 3 * slot if slot < NBLK else 3 * NBLK + 4 * (slot - NBLK)


def front_kernel(lat_ref, cols_ref, mom_ref, newmom_ref, high_ref, low_ref, packed_ref, tlt_ref, gram_ref):
    step = pl.program_id(0)
    tasks = lat_ref.shape[0]
    width = tlt_ref.shape[0]

    @pl.when(step == 0)
    def _():
        tail = lat_ref[:, width:].astype(F32)
        ids = jnp.sum(tail, axis=1, keepdims=True)
        which = lax.broadcasted_iota(jnp.int32, (tasks, tasks), 1).astype(F32)
        onehot = jnp.where(which == ids, 1.0, 0.0).astype(BF16)
        task_latent = mxu(onehot, lat_ref[:, :width])
        tlt_ref[...] = task_latent.T.astype(BF16)
        gram_ref[...] = jnp.zeros_like(gram_ref)

    for i in range(NBLK):
        rows = slice(i * BLOCK, (i + 1) * BLOCK)
        head = mxu(tlt_ref[rows, :], cols_ref[...])
        new_momentum = MOMENTUM_DECAY * mom_ref[rows, :] + head
        newmom_ref[rows, :] = new_momentum
        high, low = split(head + MOMENTUM_DECAY * new_momentum)
        high_ref[rows, :] = high
        low_ref[rows, :] = low

    def body(slot, carry):
        row, col = pair_of(slot)
        rows = pl.ds(pl.multiple_of(row * BLOCK, BLOCK), BLOCK)
        cols = pl.ds(pl.multiple_of(col * BLOCK, BLOCK), BLOCK)
        gram_ref[slot] += (
            mxu_t(high_ref[rows, :], high_ref[cols, :])
            + mxu_t(high_ref[rows, :], low_ref[cols, :])
            + mxu_t(low_ref[rows, :], high_ref[cols, :])
        )
        return carry

    lax.fori_loop(0, NPAIR, body, 0)

    @pl.when(step == pl.num_programs(0) - 1)
    def _():
        half = BLOCK // 2
        for slot in range(NPAIR):
            for at, (r, c) in enumerate(quarters(slot)):
                base = (first_of(slot) + at) * half
                packed_ref[base : base + half, :] = gram_ref[slot, r * half : (r + 1) * half, c * half : (c + 1) * half]


def front(lat, cols, momentum):
    width, count = momentum.shape
    tasks = lat.shape[0]
    grid = count // CHUNK
    return pl.pallas_call(
        front_kernel,
        grid=(grid,),
        in_specs=[
            pl.BlockSpec(lat.shape, lambda c: (0, 0)),
            pl.BlockSpec((tasks, CHUNK), lambda c: (0, c)),
            pl.BlockSpec((width, CHUNK), lambda c: (0, c)),
        ],
        out_specs=[
            pl.BlockSpec((width, CHUNK), lambda c: (0, c)),
            pl.BlockSpec((width, CHUNK), lambda c: (0, c)),
            pl.BlockSpec((width, CHUNK), lambda c: (0, c)),
            pl.BlockSpec((PACKED, 128), lambda c: (0, 0)),
        ],
        out_shape=[
            jax.ShapeDtypeStruct((width, count), F32),
            jax.ShapeDtypeStruct((width, count), BF16),
            jax.ShapeDtypeStruct((width, count), BF16),
            jax.ShapeDtypeStruct((PACKED, 128), F32),
        ],
        scratch_shapes=[pltpu.VMEM((width, tasks), BF16), pltpu.VMEM((NPAIR, BLOCK, BLOCK), F32)],
        compiler_params=pltpu.CompilerParams(vmem_limit_bytes=60 << 20),
        name="front",
    )(lat, cols, momentum)


def back_kernel(gram_ref, high_ref, low_ref, scale_ref, step_ref, inv_ref, mats_ref):
    G, M1, T, G2 = 0, 1, 2, 3

    def unpack(slot):
        half = BLOCK // 2
        base = first_of(slot) * half
        part = [gram_ref[base + at * half : base + (at + 1) * half, :] for at in range(len(quarters(slot)))]
        if slot < NBLK:
            part = [part[0], part[1], part[1].T, part[2]]
        top = jnp.concatenate(part[:2], axis=1)
        return jnp.concatenate([top, jnp.concatenate(part[2:], axis=1)], axis=0)

    def store(which, row, col, value):
        high, low = split(value)
        rows = pl.ds(pl.multiple_of(row * BLOCK, BLOCK), BLOCK)
        cols = pl.ds(pl.multiple_of(col * BLOCK, BLOCK), BLOCK)
        mats_ref[which, 0, col, rows, :] = high
        mats_ref[which, 1, col, rows, :] = low
        flipped, flipped_low = split(value.T)
        mats_ref[which, 0, row, cols, :] = flipped
        mats_ref[which, 1, row, cols, :] = flipped_low

    def eye(row, col):
        r = lax.broadcasted_iota(jnp.int32, (BLOCK, BLOCK), 0)
        c = lax.broadcasted_iota(jnp.int32, (BLOCK, BLOCK), 1)
        return jnp.where((r == c) & (row == col), 1.0, 0.0)

    def product(left, right, row, col):
        rows = pl.ds(pl.multiple_of(row * BLOCK, BLOCK), BLOCK)
        total = None
        for k in range(NBLK):
            ks = slice(k * BLOCK, (k + 1) * BLOCK)
            lh, ll = mats_ref[left, 0, k, rows, :], mats_ref[left, 1, k, rows, :]
            rh, rl = mats_ref[right, 0, col, ks, :], mats_ref[right, 1, col, ks, :]
            term = mxu(lh, rh) + mxu(lh, rl) + mxu(ll, rh)
            total = term if total is None else total + term
        return total

    def stage(left, right, dest, finish):
        def body(slot, carry):
            row, col = pair_of(slot)
            store(dest, row, col, finish(slot, row, col, product(left, right, row, col)))
            return carry

        lax.fori_loop(0, NPAIR, body, 0)

    @pl.when(pl.program_id(0) == 0)
    def _():
        r = lax.broadcasted_iota(jnp.int32, (BLOCK, BLOCK), 0)
        c = lax.broadcasted_iota(jnp.int32, (BLOCK, BLOCK), 1)
        diagonal = unpack(0) + unpack(1) + unpack(2) + unpack(3)
        picked = jnp.where(r == c, diagonal, 0.0)
        squares = jnp.sum(jnp.sum(picked, axis=1, keepdims=True), axis=0, keepdims=True)
        inverse = 1.0 / (jnp.sqrt(squares) + EPSILON)
        inv_ref[...] = jnp.broadcast_to(inverse, inv_ref.shape)

        for slot in range(NPAIR):
            row = slot % NBLK
            store(G, row, (row + slot // NBLK) % NBLK, (unpack(slot) * inverse) * inverse)

        def newton(which):
            def finish(slot, row, col, value):
                rows = pl.ds(pl.multiple_of(row * BLOCK, BLOCK), BLOCK)
                own = mats_ref[which, 0, col, rows, :].astype(F32) + mats_ref[which, 1, col, rows, :].astype(F32)
                return NEWTON_A * eye(row, col) + NEWTON_B * own + NEWTON_C * value

            return finish

        plain = lambda slot, row, col, value: value
        stage(G, G, M1, newton(G))
        stage(G, M1, T, plain)
        stage(T, M1, G2, plain)
        stage(G2, G2, G, newton(G2))
        stage(G, M1, T, plain)

    width = CHUNK // 128
    factor = [
        scale_ref[pl.ds(pl.program_id(0) * width + at, 1), :] * (math.sqrt(OUT) * inv_ref[0:1, 0:1])
        for at in range(width)
    ]
    for i in range(NBLK):
        rows = slice(i * BLOCK, (i + 1) * BLOCK)
        total = None
        for k in range(NBLK):
            ks = slice(k * BLOCK, (k + 1) * BLOCK)
            mh, ml = mats_ref[T, 0, k, rows, :], mats_ref[T, 1, k, rows, :]
            term = mxu(mh, high_ref[ks, :]) + mxu(mh, low_ref[ks, :]) + mxu(ml, high_ref[ks, :])
            total = term if total is None else total + term
        for at in range(width):
            lanes = slice(at * 128, (at + 1) * 128)
            step_ref[rows, lanes] = total[:, lanes] * factor[at]


def back(gram, high, low, scale):
    width, count = high.shape
    return pl.pallas_call(
        back_kernel,
        grid=(count // CHUNK,),
        in_specs=[
            pl.BlockSpec(gram.shape, lambda c: (0, 0)),
            pl.BlockSpec((width, CHUNK), lambda c: (0, c)),
            pl.BlockSpec((width, CHUNK), lambda c: (0, c)),
            pl.BlockSpec(scale.shape, lambda c: (0, 0)),
        ],
        out_specs=pl.BlockSpec((width, CHUNK), lambda c: (0, c)),
        out_shape=jax.ShapeDtypeStruct((width, count), F32),
        scratch_shapes=[
            pltpu.VMEM((8, 128), F32),
            pltpu.VMEM((4, 2, NBLK, width, BLOCK), BF16),
        ],
        compiler_params=pltpu.CompilerParams(vmem_limit_bytes=60 << 20),
        name="back",
    )(gram, high, low, scale)


def per_device(factor_grads, latents, task_ids, offsets, target_scale, momentum):
    columns, lat, column_scale = exchange(factor_grads, latents, task_ids, offsets, target_scale)
    columns = columns.reshape(-1, columns.shape[-1])
    lat = lat.reshape(-1, lat.shape[-1])
    new_momentum, high, low, gram = front(lat, columns, momentum)
    return new_momentum, back(reduce_gram(gram), high, low, column_scale)


def solution(mesh):
    placed = (
        P(("gx", "gy"), None),
        P(("gx", "gy"), None),
        P(("gx", "gy")),
        P(),
        P(),
        P(None, ("gx", "gy")),
    )
    return jax.shard_map(
        per_device,
        mesh=mesh,
        in_specs=placed,
        out_specs=(P(None, ("gx", "gy")), P(None, ("gx", "gy"))),
        check_vma=False,
    )
```

```python
import math

import jax
import jax.numpy as jnp
from jax import lax
from jax.experimental import pallas as pl
from jax.experimental.pallas import tpu as pltpu
from jax.sharding import PartitionSpec as P

OUT = 196608
MOMENTUM_DECAY = 0.95
EPSILON = 1e-07
NEWTON_A = 3.4445
NEWTON_B = -4.775
NEWTON_C = 2.0315

BLOCK = 256
NBLK = 4
NPAIR = 10
CHUNK = 512
PACKED = 36 * 128
F32 = jnp.float32
BF16 = jnp.bfloat16
MESH = pl.DeviceIdType.MESH


def place():
    gx = lax.axis_index("gx")
    gy = lax.axis_index("gy")
    return lax.div(gx, 4), lax.rem(gx, 4), lax.div(gy, 2), lax.rem(gy, 2)


def peer_of(where, axis, hop):
    x, z, y, core = where
    if axis == 0:
        x = lax.rem(x + hop, 4)
    elif axis == 1:
        y = lax.rem(y + hop, 4)
    elif axis == 2:
        z = lax.rem(z + hop, 4)
    else:
        core = 1 - core
    return (x * 4 + z, y * 2 + core)


def split(value):
    high = value.astype(BF16)
    return high, (value - high.astype(F32)).astype(BF16)


def mxu(left, right):
    return lax.dot_general(left, right, (((1,), (0,)), ((), ())), preferred_element_type=F32)


def mxu_t(left, right):
    return lax.dot_general(left, right, (((1,), (1,)), ((), ())), preferred_element_type=F32)


def pair_of(slot):
    row = lax.rem(slot, NBLK)
    col = lax.rem(row + lax.div(slot, NBLK), NBLK)
    return row, col


def quarters(slot):
    return ((0, 0), (0, 1), (1, 1)) if slot < NBLK else ((0, 0), (0, 1), (1, 0), (1, 1))


def first_of(slot):
    return 3 * slot if slot < NBLK else 3 * NBLK + 4 * (slot - NBLK)


def gather_kernel(grads_ref, lat_ref, ids_ref, offsets_ref, scales_ref, mom_ref,
                  out_ref, head_ref, scale_ref,
                  own_ref, cols_ref, lats_ref, tlt_ref, moms_ref, heads_ref, high_ref, low_ref, acc_ref,
                  packed_ref, core_ref, half_ref, got1_ref, sum1_ref, got2_ref, sum2_ref, got3_ref,
                  gs, gr, own_sem, ms, hs, a1, b1, a2, b2, a3, b3, a4, b4,
                  cs, cr, s1, r1, s2, r2, s3, r3, s4, r4, s5, r5, s6, r6):
    where = place()
    x, z, y, core = where
    coord = (x, y, z)
    parts, total, rows, chunk = cols_ref.shape
    count = parts * chunk
    width = lat_ref.shape[1]
    tasks = total * rows
    me = lax.axis_index("gx") * 8 + lax.axis_index("gy")
    barrier = pltpu.get_barrier_semaphore()
    hops = (2, 1, 3)

    def device(to):
        return (lax.div(to, 8), lax.rem(to, 8))

    def greet(k, carry):
        to = lax.rem(me + lax.rem(k * 37, total), total)
        pl.semaphore_signal(barrier, inc=1, device_id=device(to), device_id_type=MESH)
        return carry

    lax.fori_loop(1, total, greet, 0)

    loads = []
    for q in range(parts):
        load = pltpu.make_async_copy(mom_ref.at[:, q * chunk : (q + 1) * chunk], moms_ref.at[q], ms.at[q])
        load.start()
        loads.append(load)

    own_ref[:, :width] = lat_ref[...]
    at_row = lax.broadcasted_iota(jnp.int32, (rows, 128), 0)
    at_lane = lax.broadcasted_iota(jnp.int32, (rows, 128), 1)
    ids = jnp.zeros((rows, 128), jnp.int32)
    for r in range(rows):
        ids = jnp.where(at_row == r, ids_ref[r], ids)
    fine = jnp.bitwise_and(ids, 15)
    tail = jnp.where(at_lane == 0, ids - fine, jnp.where(at_lane == 1, fine, 0))
    own_ref[:, width:] = tail.astype(F32).astype(BF16)

    column = me * count + 128 * lax.broadcasted_iota(jnp.int32, scale_ref.shape, 0)
    column = column + lax.broadcasted_iota(jnp.int32, scale_ref.shape, 1)

    def level(t, value):
        return jnp.where(column >= offsets_ref[t], scales_ref[t], value)

    scale_ref[...] = lax.fori_loop(0, offsets_ref.shape[0], level, jnp.zeros(scale_ref.shape, F32))

    pl.semaphore_wait(barrier, total - 1)

    started = []

    def remote(src, dst, ssem, rsem, dev):
        copy = pltpu.make_async_remote_copy(
            src_ref=src, dst_ref=dst, send_sem=ssem, recv_sem=rsem, device_id=dev, device_id_type=MESH)
        copy.start()
        started.append(copy)
        return copy

    def arrived(copies):
        for copy in copies:
            copy.wait_recv()

    keep = pltpu.make_async_copy(own_ref, lats_ref.at[x, z, y, core], own_sem)
    keep.start()
    first = [remote(own_ref, lats_ref.at[x, z, y, core], a1.at[k - 1], b1.at[k - 1], peer_of(where, 1, k)) for k in hops]

    def columns_of(owner, q):
        return grads_ref.at[:, pl.ds(pl.multiple_of(owner * count + q * chunk, 128), chunk)]

    for q in range(parts):
        pltpu.make_async_copy(columns_of(me, q), cols_ref.at[q, me], gr.at[q]).start()

    def send(q, low, high):
        def body(k, carry):
            to = lax.rem(me + lax.rem(k * 37, total), total)
            pltpu.make_async_remote_copy(
                src_ref=columns_of(to, q), dst_ref=cols_ref.at[q, me], send_sem=gs.at[q], recv_sem=gr.at[q],
                device_id=device(to), device_id_type=MESH).start()
            return carry

        lax.fori_loop(low, high, body, 0)

    send(0, 1, 64)
    keep.wait()
    arrived(first)
    part = lats_ref.at[x, z, :, core]
    second = [remote(part, part, a2.at[k - 1], b2.at[k - 1], peer_of(where, 2, k)) for k in hops]
    send(0, 64, total)
    arrived(second)
    part = lats_ref.at[x, :, :, core]
    third = [remote(part, part, a3.at[k - 1], b3.at[k - 1], peer_of(where, 0, k)) for k in hops]
    for q in range(1, parts):
        send(q, 1, total)
    arrived(third)
    part = lats_ref.at[:, :, :, core]
    arrived([remote(part, part, a4, b4, peer_of(where, 3, 1))])

    def flat(value):
        value = value.astype(F32).reshape(total // 2, 2, rows, value.shape[-1])
        return jnp.concatenate([value[:, 0], value[:, 1]], axis=1).reshape(tasks, value.shape[-1])

    lat = flat(lats_ref[...].reshape(total, rows, width + 128))
    task = jnp.sum(lat[:, width:], axis=1, keepdims=True)
    which = lax.broadcasted_iota(jnp.int32, (tasks, tasks), 1).astype(F32)
    onehot = jnp.where(which == task, 1.0, 0.0).astype(BF16)
    tlt_ref[...] = mxu(onehot, lat[:, :width].astype(BF16)).T.astype(BF16)
    acc_ref[...] = jnp.zeros_like(acc_ref)

    def gram(low, high):
        def body(slot, carry):
            row, col = pair_of(slot)
            top = pl.ds(pl.multiple_of(row * BLOCK, BLOCK), BLOCK)
            side = pl.ds(pl.multiple_of(col * BLOCK, BLOCK), BLOCK)
            acc_ref[slot] += (
                mxu_t(high_ref[top, :], high_ref[side, :])
                + mxu_t(high_ref[top, :], low_ref[side, :])
                + mxu_t(low_ref[top, :], high_ref[side, :])
            )
            return carry

        lax.fori_loop(low, high, body, 0)

    def blend(q):
        pltpu.make_async_copy(cols_ref.at[q], cols_ref.at[q], gr.at[q]).wait()
        loads[q].wait()
        cols = flat(cols_ref[q]).astype(BF16)
        for i in range(NBLK):
            at = slice(i * BLOCK, (i + 1) * BLOCK)
            head = mxu(tlt_ref[at, :], cols)
            heads_ref[q, at, :] = head
            new_momentum = MOMENTUM_DECAY * moms_ref[q, at, :] + head
            high, low = split(head + MOMENTUM_DECAY * new_momentum)
            high_ref[at, :] = high
            low_ref[at, :] = low
        store = pltpu.make_async_copy(heads_ref.at[q], head_ref.at[:, q * chunk : (q + 1) * chunk], hs.at[q])
        store.start()
        return store

    stores = []
    for q in range(parts - 1):
        stores.append(blend(q))
        gram(0, NPAIR)
    stores.append(blend(parts - 1))

    other = 1 - core
    size = packed_ref.shape[1]
    halfs, quart, piece = size // 2, size // 8, size // 32

    def span(index, length):
        return pl.ds(pl.multiple_of(index * length, 8), length)

    cored = []
    edges = (0, NBLK, NBLK + 3, NPAIR)
    for r in range(3):
        gram(edges[r], edges[r + 1])
        for slot in range(edges[r], edges[r + 1]):
            small = BLOCK // 2
            for at, (i, j) in enumerate(quarters(slot)):
                base = (first_of(slot) + at) * small - r * size
                packed_ref[r, base : base + small, :] = acc_ref[slot, i * small : (i + 1) * small, j * small : (j + 1) * small]
        cored.append(remote(packed_ref.at[r, span(other, halfs)], core_ref.at[r], cs.at[r], cr.at[r], peer_of(where, 3, 1)))

    phase = []
    for r in range(3):
        cored[r].wait_recv()
        half_ref[r] = packed_ref[r, span(core, halfs), :] + core_ref[r]
        phase.append([
            remote(half_ref.at[r, span(lax.rem(coord[r] + k, 4), quart)], got1_ref.at[r, k - 1],
                   s1.at[r, k - 1], r1.at[r, k - 1], peer_of(where, r, k)) for k in hops])
    phase2 = []
    for r in range(3):
        b = (r + 1) % 3
        arrived(phase[r])
        sum1_ref[r] = (half_ref[r, span(coord[r], quart), :] + got1_ref[r, 0]) + (got1_ref[r, 1] + got1_ref[r, 2])
        phase2.append([
            remote(sum1_ref.at[r, span(lax.rem(coord[b] + k, 4), piece)], got2_ref.at[r, k - 1],
                   s2.at[r, k - 1], r2.at[r, k - 1], peer_of(where, b, k)) for k in hops])
    phase3 = []
    for r in range(3):
        b, d = (r + 1) % 3, (r + 2) % 3
        arrived(phase2[r])
        sum2_ref[r] = (sum1_ref[r, span(coord[b], piece), :] + got2_ref[r, 0]) + (got2_ref[r, 1] + got2_ref[r, 2])
        phase3.append([
            remote(sum2_ref.at[r], got3_ref.at[r, k - 1], s3.at[r, k - 1], r3.at[r, k - 1], peer_of(where, d, k))
            for k in hops])
    phase4 = []
    for r in range(3):
        b = (r + 1) % 3
        arrived(phase3[r])
        mine = span(core * 16 + coord[r] * 4 + coord[b], piece)
        out_ref[r, mine, :] = (sum2_ref[r] + got3_ref[r, 0]) + (got3_ref[r, 1] + got3_ref[r, 2])
        own = out_ref.at[r, mine]
        phase4.append([remote(own, own, s4.at[r, k - 1], r4.at[r, k - 1], peer_of(where, b, k)) for k in hops])
    phase5 = []
    for r in range(3):
        arrived(phase4[r])
        own = out_ref.at[r, span(core * 4 + coord[r], quart)]
        phase5.append([remote(own, own, s5.at[r, k - 1], r5.at[r, k - 1], peer_of(where, r, k)) for k in hops])
    last = []
    for r in range(3):
        arrived(phase5[r])
        own = out_ref.at[r, span(core, halfs)]
        last.append(remote(own, own, s6.at[r], r6.at[r], peer_of(where, 3, 1)))
    arrived(last)
    for copy in started:
        copy.wait_send()
    for q in range(parts):
        sent = cols_ref.at[q, pl.ds(0, total - 1)]
        pltpu.make_async_copy(sent, sent, gs.at[q]).wait()
        stores[q].wait()


def gather(grads, lat, ids, offsets, scales, momentum):
    rows, latent = lat.shape
    width, count = momentum.shape
    total = grads.shape[1] // count
    parts = count // CHUNK
    tasks = rows * total
    size = PACKED // 3
    dma = pltpu.SemaphoreType.DMA
    smem = pl.BlockSpec(memory_space=pltpu.SMEM)
    vmem = pl.BlockSpec(memory_space=pltpu.VMEM)
    anywhere = pl.BlockSpec(memory_space=pl.ANY)
    return pl.pallas_call(
        gather_kernel,
        in_specs=[anywhere, vmem, smem, smem, smem, anywhere],
        out_specs=[vmem, anywhere, vmem],
        out_shape=[
            jax.ShapeDtypeStruct((3, size, 128), F32),
            jax.ShapeDtypeStruct((width, count), F32),
            jax.ShapeDtypeStruct((count // 128, 128), F32),
        ],
        scratch_shapes=[
            pltpu.VMEM((rows, latent + 128), BF16),
            pltpu.VMEM((parts, total, rows, CHUNK), BF16),
            pltpu.VMEM((4, 4, 4, 2, rows, latent + 128), BF16),
            pltpu.VMEM((width, tasks), BF16),
            pltpu.VMEM((parts, width, CHUNK), F32),
            pltpu.VMEM((parts, width, CHUNK), F32),
            pltpu.VMEM((width, CHUNK), BF16),
            pltpu.VMEM((width, CHUNK), BF16),
            pltpu.VMEM((NPAIR, BLOCK, BLOCK), F32),
            pltpu.VMEM((3, size, 128), F32),
            pltpu.VMEM((3, size // 2, 128), F32),
            pltpu.VMEM((3, size // 2, 128), F32),
            pltpu.VMEM((3, 3, size // 8, 128), F32),
            pltpu.VMEM((3, size // 8, 128), F32),
            pltpu.VMEM((3, 3, size // 32, 128), F32),
            pltpu.VMEM((3, size // 32, 128), F32),
            pltpu.VMEM((3, 3, size // 32, 128), F32),
            dma((parts,)), dma((parts,)), dma, dma((parts,)), dma((parts,)),
        ]
        + [dma((3,))] * 6 + [dma, dma, dma((3,)), dma((3,))]
        + [dma((3, 3))] * 10 + [dma((3,)), dma((3,))],
        compiler_params=pltpu.CompilerParams(collective_id=1, has_side_effects=True, vmem_limit_bytes=60 << 20),
        name="gather",
    )(grads, lat, ids, offsets, scales, momentum)


def back_kernel(gram_ref, head_ref, mom_ref, scale_ref, newmom_ref, step_ref, inv_ref, mats_ref, high_ref, low_ref):
    G, M1, T, G2 = 0, 1, 2, 3

    def unpack(slot):
        half = BLOCK // 2
        base = first_of(slot) * half
        part = [gram_ref[base + at * half : base + (at + 1) * half, :] for at in range(len(quarters(slot)))]
        if slot < NBLK:
            part = [part[0], part[1], part[1].T, part[2]]
        top = jnp.concatenate(part[:2], axis=1)
        return jnp.concatenate([top, jnp.concatenate(part[2:], axis=1)], axis=0)

    def store(which, row, col, value):
        high, low = split(value)
        rows = pl.ds(pl.multiple_of(row * BLOCK, BLOCK), BLOCK)
        cols = pl.ds(pl.multiple_of(col * BLOCK, BLOCK), BLOCK)
        mats_ref[which, 0, col, rows, :] = high
        mats_ref[which, 1, col, rows, :] = low
        flipped, flipped_low = split(value.T)
        mats_ref[which, 0, row, cols, :] = flipped
        mats_ref[which, 1, row, cols, :] = flipped_low

    def eye(row, col):
        r = lax.broadcasted_iota(jnp.int32, (BLOCK, BLOCK), 0)
        c = lax.broadcasted_iota(jnp.int32, (BLOCK, BLOCK), 1)
        return jnp.where((r == c) & (row == col), 1.0, 0.0)

    def product(left, right, row, col):
        rows = pl.ds(pl.multiple_of(row * BLOCK, BLOCK), BLOCK)
        total = None
        for k in range(NBLK):
            ks = slice(k * BLOCK, (k + 1) * BLOCK)
            lh, ll = mats_ref[left, 0, k, rows, :], mats_ref[left, 1, k, rows, :]
            rh, rl = mats_ref[right, 0, col, ks, :], mats_ref[right, 1, col, ks, :]
            term = mxu(lh, rh) + mxu(lh, rl) + mxu(ll, rh)
            total = term if total is None else total + term
        return total

    def stage(left, right, dest, finish):
        def body(slot, carry):
            row, col = pair_of(slot)
            store(dest, row, col, finish(slot, row, col, product(left, right, row, col)))
            return carry

        lax.fori_loop(0, NPAIR, body, 0)

    @pl.when(pl.program_id(0) == 0)
    def _():
        r = lax.broadcasted_iota(jnp.int32, (BLOCK, BLOCK), 0)
        c = lax.broadcasted_iota(jnp.int32, (BLOCK, BLOCK), 1)
        diagonal = unpack(0) + unpack(1) + unpack(2) + unpack(3)
        picked = jnp.where(r == c, diagonal, 0.0)
        squares = jnp.sum(jnp.sum(picked, axis=1, keepdims=True), axis=0, keepdims=True)
        inverse = 1.0 / (jnp.sqrt(squares) + EPSILON)
        inv_ref[...] = jnp.broadcast_to(inverse, inv_ref.shape)

        for slot in range(NPAIR):
            row = slot % NBLK
            store(G, row, (row + slot // NBLK) % NBLK, (unpack(slot) * inverse) * inverse)

        def newton(which):
            def finish(slot, row, col, value):
                rows = pl.ds(pl.multiple_of(row * BLOCK, BLOCK), BLOCK)
                own = mats_ref[which, 0, col, rows, :].astype(F32) + mats_ref[which, 1, col, rows, :].astype(F32)
                return NEWTON_A * eye(row, col) + NEWTON_B * own + NEWTON_C * value

            return finish

        plain = lambda slot, row, col, value: value
        stage(G, G, M1, newton(G))
        stage(G, M1, T, plain)
        stage(T, M1, G2, plain)
        stage(G2, G2, G, newton(G2))
        stage(G, M1, T, plain)

    new_momentum = MOMENTUM_DECAY * mom_ref[...] + head_ref[...]
    newmom_ref[...] = new_momentum
    high_ref[...], low_ref[...] = split(head_ref[...] + MOMENTUM_DECAY * new_momentum)
    width = CHUNK // 128
    factor = [
        scale_ref[pl.ds(pl.program_id(0) * width + at, 1), :] * (math.sqrt(OUT) * inv_ref[0:1, 0:1])
        for at in range(width)
    ]
    for i in range(NBLK):
        rows = slice(i * BLOCK, (i + 1) * BLOCK)
        total = None
        for k in range(NBLK):
            ks = slice(k * BLOCK, (k + 1) * BLOCK)
            mh, ml = mats_ref[T, 0, k, rows, :], mats_ref[T, 1, k, rows, :]
            term = mxu(mh, high_ref[ks, :]) + mxu(mh, low_ref[ks, :]) + mxu(ml, high_ref[ks, :])
            total = term if total is None else total + term
        for at in range(width):
            lanes = slice(at * 128, (at + 1) * 128)
            step_ref[rows, lanes] = total[:, lanes] * factor[at]


def back(gram, head, momentum, scale):
    width, count = head.shape
    return pl.pallas_call(
        back_kernel,
        grid=(count // CHUNK,),
        in_specs=[
            pl.BlockSpec(gram.shape, lambda c: (0, 0)),
            pl.BlockSpec((width, CHUNK), lambda c: (0, c)),
            pl.BlockSpec((width, CHUNK), lambda c: (0, c)),
            pl.BlockSpec(scale.shape, lambda c: (0, 0)),
        ],
        out_specs=[pl.BlockSpec((width, CHUNK), lambda c: (0, c))] * 2,
        out_shape=[jax.ShapeDtypeStruct((width, count), F32)] * 2,
        scratch_shapes=[
            pltpu.VMEM((8, 128), F32),
            pltpu.VMEM((4, 2, NBLK, width, BLOCK), BF16),
            pltpu.VMEM((width, CHUNK), BF16),
            pltpu.VMEM((width, CHUNK), BF16),
        ],
        compiler_params=pltpu.CompilerParams(vmem_limit_bytes=60 << 20),
        name="back",
    )(gram, head, momentum, scale)


def per_device(factor_grads, latents, task_ids, offsets, target_scale, momentum):
    gram, head, column_scale = gather(factor_grads, latents, task_ids, offsets, target_scale, momentum)
    new_momentum, step = back(gram.reshape(-1, 128), head, momentum, column_scale)
    return new_momentum, step


def solution(mesh):
    placed = (
        P(("gx", "gy"), None),
        P(("gx", "gy"), None),
        P(("gx", "gy")),
        P(),
        P(),
        P(None, ("gx", "gy")),
    )
    return jax.shard_map(
        per_device,
        mesh=mesh,
        in_specs=placed,
        out_specs=(P(None, ("gx", "gy")), P(None, ("gx", "gy"))),
        check_vma=False,
    )
```

```python
import math

import jax
import jax.numpy as jnp
from jax import lax
from jax.experimental import pallas as pl
from jax.experimental.pallas import tpu as pltpu
from jax.sharding import PartitionSpec as P

OUT = 196608
MOMENTUM_DECAY = 0.95
EPSILON = 1e-07
NEWTON_A = 3.4445
NEWTON_B = -4.775
NEWTON_C = 2.0315

BLOCK = 256
NBLK = 4
NPAIR = 10
CHUNK = 512
WIDTHS = (512, 512, 512)
PACKED = 36 * 128
F32 = jnp.float32
BF16 = jnp.bfloat16
MESH = pl.DeviceIdType.MESH


def place():
    gx = lax.axis_index("gx")
    gy = lax.axis_index("gy")
    return lax.div(gx, 4), lax.rem(gx, 4), lax.div(gy, 2), lax.rem(gy, 2)


def peer_of(where, axis, hop):
    x, z, y, core = where
    if axis == 0:
        x = lax.rem(x + hop, 4)
    elif axis == 1:
        y = lax.rem(y + hop, 4)
    elif axis == 2:
        z = lax.rem(z + hop, 4)
    else:
        core = 1 - core
    return (x * 4 + z, y * 2 + core)


def split(value):
    high = value.astype(BF16)
    return high, (value - high.astype(F32)).astype(BF16)


def mxu(left, right):
    return lax.dot_general(left, right, (((1,), (0,)), ((), ())), preferred_element_type=F32)


def mxu_t(left, right):
    return lax.dot_general(left, right, (((1,), (1,)), ((), ())), preferred_element_type=F32)


def pair_of(slot):
    row = lax.rem(slot, NBLK)
    col = lax.rem(row + lax.div(slot, NBLK), NBLK)
    return row, col


def gather_kernel(grads_ref, lat_ref, ids_ref, offsets_ref, scales_ref, mom_ref,
                  final_ref, head_ref, scale_ref,
                  own_ref, cols_refs, lats_ref, tlt_ref, moms_ref, heads_ref, high_ref, low_ref, acc_ref,
                  packed_ref, core_ref, half_ref, got1_ref, sum1_ref, got2_ref, sum2_ref, got3_ref,
                  sums_ref, mats_ref, trace_ref,
                  gs, gr, own_sem, ms, hs, a1, b1, a2, b2, a3, b3, a4, b4,
                  cs, cr, s1, r1, s2, r2, s3, r3, s4, r4, s5, r5, ts, tr, ps, pr):
    where = place()
    x, z, y, core = where
    coord = (x, y, z)
    parts = len(cols_refs)
    total, rows = cols_refs[0].shape[:2]
    widths = [ref.shape[2] for ref in cols_refs]
    begin = [sum(widths[:q]) for q in range(parts)]
    count = sum(widths)
    width = lat_ref.shape[1]
    tasks = total * rows
    me = lax.axis_index("gx") * 8 + lax.axis_index("gy")
    barrier = pltpu.get_barrier_semaphore()
    hops = (2, 1, 3)

    def device(to):
        return (lax.div(to, 8), lax.rem(to, 8))

    def greet(k, carry):
        to = lax.rem(me + lax.rem(k * 37, total), total)
        pl.semaphore_signal(barrier, inc=1, device_id=device(to), device_id_type=MESH)
        return carry

    lax.fori_loop(1, total, greet, 0)

    loads = []
    for q in range(parts):
        lanes = slice(begin[q], begin[q] + widths[q])
        load = pltpu.make_async_copy(mom_ref.at[:, lanes], moms_ref.at[:, lanes], ms.at[q])
        load.start()
        loads.append(load)

    own_ref[:, :width] = lat_ref[...]
    at_row = lax.broadcasted_iota(jnp.int32, (rows, 128), 0)
    at_lane = lax.broadcasted_iota(jnp.int32, (rows, 128), 1)
    ids = jnp.zeros((rows, 128), jnp.int32)
    for r in range(rows):
        ids = jnp.where(at_row == r, ids_ref[r], ids)
    fine = jnp.bitwise_and(ids, 15)
    tail = jnp.where(at_lane == 0, ids - fine, jnp.where(at_lane == 1, fine, 0))
    own_ref[:, width:] = tail.astype(F32).astype(BF16)

    column = me * count + 128 * lax.broadcasted_iota(jnp.int32, scale_ref.shape, 0)
    column = column + lax.broadcasted_iota(jnp.int32, scale_ref.shape, 1)

    def level(t, value):
        return jnp.where(column >= offsets_ref[t], scales_ref[t], value)

    scale_ref[...] = lax.fori_loop(0, offsets_ref.shape[0], level, jnp.zeros(scale_ref.shape, F32))

    pl.semaphore_wait(barrier, total - 1)

    started = []

    def remote(src, dst, ssem, rsem, dev):
        copy = pltpu.make_async_remote_copy(
            src_ref=src, dst_ref=dst, send_sem=ssem, recv_sem=rsem, device_id=dev, device_id_type=MESH)
        copy.start()
        started.append(copy)
        return copy

    def arrived(copies):
        for copy in copies:
            copy.wait_recv()

    keep = pltpu.make_async_copy(own_ref, lats_ref.at[x, z, y, core], own_sem)
    keep.start()
    third = (width + 128) // 3
    orders = ((1, 2, 0), (2, 0, 1), (0, 1, 2))

    def region(p, level):
        full = orders[p][:level]
        at = tuple(slice(None) if axis in full else coord[axis] for axis in (0, 2, 1))
        return lats_ref.at[at + (core, slice(None), slice(p * third, (p + 1) * third))]

    def spread(level, ssem, rsem):
        copies = []
        for p in range(3):
            source = own_ref.at[:, p * third : (p + 1) * third] if level == 0 else region(p, level)
            for k in hops:
                copies.append(remote(source, region(p, level), ssem.at[p, k - 1], rsem.at[p, k - 1],
                                     peer_of(where, orders[p][level], k)))
        return copies

    first = spread(0, a1, b1)

    def columns_of(owner, q):
        return grads_ref.at[:, pl.ds(pl.multiple_of(owner * count + begin[q], 128), widths[q])]

    for q in range(parts):
        pltpu.make_async_copy(columns_of(me, q), cols_refs[q].at[me], gr.at[q]).start()

    def send(q, low, high):
        def body(k, carry):
            to = lax.rem(me + lax.rem(k * 37, total), total)
            pltpu.make_async_remote_copy(
                src_ref=columns_of(to, q), dst_ref=cols_refs[q].at[me], send_sem=gs.at[q], recv_sem=gr.at[q],
                device_id=device(to), device_id_type=MESH).start()
            return carry

        lax.fori_loop(low, high, body, 0)

    send(0, 1, 48)
    keep.wait()
    arrived(first)
    second = spread(1, a2, b2)
    send(0, 48, 88)
    arrived(second)
    rest = spread(2, a3, b3)
    send(0, 88, total)
    for q in range(1, parts):
        send(q, 1, total)
    arrived(rest)
    part = lats_ref.at[:, :, :, core]
    arrived([remote(part, part, a4, b4, peer_of(where, 3, 1))])

    def flat(value):
        value = value.astype(F32).reshape(total // 2, 2, rows, value.shape[-1])
        return jnp.concatenate([value[:, 0], value[:, 1]], axis=1).reshape(tasks, value.shape[-1])

    lat = flat(lats_ref[...].reshape(total, rows, width + 128))
    task = jnp.sum(lat[:, width:], axis=1, keepdims=True)
    which = lax.broadcasted_iota(jnp.int32, (tasks, tasks), 1).astype(F32)
    onehot = jnp.where(which == task, 1.0, 0.0).astype(BF16)
    tlt_ref[...] = mxu(onehot, lat[:, :width].astype(BF16)).T.astype(BF16)
    acc_ref[...] = jnp.zeros_like(acc_ref)

    def gram(used, low, high):
        def body(slot, carry):
            row, col = pair_of(slot)
            top = pl.ds(pl.multiple_of(row * BLOCK, BLOCK), BLOCK)
            side = pl.ds(pl.multiple_of(col * BLOCK, BLOCK), BLOCK)
            acc_ref[slot] += (
                mxu_t(high_ref[top, :used], high_ref[side, :used])
                + mxu_t(high_ref[top, :used], low_ref[side, :used])
                + mxu_t(low_ref[top, :used], high_ref[side, :used])
            )
            return carry

        lax.fori_loop(low, high, body, 0)

    def blend(q):
        pltpu.make_async_copy(cols_refs[q], cols_refs[q], gr.at[q]).wait()
        loads[q].wait()
        cols = flat(cols_refs[q][...]).astype(BF16)
        lanes = slice(begin[q], begin[q] + widths[q])
        for i in range(NBLK):
            at = slice(i * BLOCK, (i + 1) * BLOCK)
            head = mxu(tlt_ref[at, :], cols)
            heads_ref[at, lanes] = head
            new_momentum = MOMENTUM_DECAY * moms_ref[at, lanes] + head
            high, low = split(head + MOMENTUM_DECAY * new_momentum)
            high_ref[at, : widths[q]] = high
            low_ref[at, : widths[q]] = low
        store = pltpu.make_async_copy(heads_ref.at[:, lanes], head_ref.at[:, lanes], hs.at[q])
        store.start()
        return store

    stores = []
    for q in range(parts - 1):
        stores.append(blend(q))
        gram(widths[q], 0, NPAIR)
    stores.append(blend(parts - 1))

    other = 1 - core
    size = packed_ref.shape[1]
    halfs, quart, piece = size // 2, size // 8, size // 32
    small = BLOCK // 2

    def span(index, length):
        return pl.ds(pl.multiple_of(index * length, 8), length)

    cored = []
    groups = (((0, 4),), ((4, 6), (7, 9)), ((6, 7), (9, 10)))
    every = tuple((i, j) for i in range(2) for j in range(2))
    layout = (
        tuple((slot, q) for slot in range(NBLK) for q in ((0, 0), (0, 1), (1, 1))),
        tuple((4, q) for q in every) + tuple((5, q) for q in every[:2])
        + tuple((7, q) for q in every) + tuple((8, q) for q in every[:2]),
        tuple((6, q) for q in every) + tuple((5, q) for q in every[2:])
        + tuple((9, q) for q in every) + tuple((8, q) for q in every[2:]),
    )
    for r in range(3):
        for low, high in groups[r]:
            gram(widths[-1], low, high)
        for at, (slot, (i, j)) in enumerate(layout[r]):
            packed_ref[r, at * small : (at + 1) * small, :] = acc_ref[slot, i * small : (i + 1) * small, j * small : (j + 1) * small]
        cored.append(remote(packed_ref.at[r, span(other, halfs)], core_ref.at[r], cs.at[r], cr.at[r], peer_of(where, 3, 1)))

    phase = []
    for r in range(3):
        cored[r].wait_recv()
        half_ref[r] = packed_ref[r, span(core, halfs), :] + core_ref[r]
        phase.append([
            remote(half_ref.at[r, span(lax.rem(coord[r] + k, 4), quart)], got1_ref.at[r, k - 1],
                   s1.at[r, k - 1], r1.at[r, k - 1], peer_of(where, r, k)) for k in hops])
    phase2 = []
    for r in range(3):
        b = (r + 1) % 3
        arrived(phase[r])
        sum1_ref[r] = (half_ref[r, span(coord[r], quart), :] + got1_ref[r, 0]) + (got1_ref[r, 1] + got1_ref[r, 2])
        phase2.append([
            remote(sum1_ref.at[r, span(lax.rem(coord[b] + k, 4), piece)], got2_ref.at[r, k - 1],
                   s2.at[r, k - 1], r2.at[r, k - 1], peer_of(where, b, k)) for k in hops])
    phase3 = []
    for r in range(3):
        b, d = (r + 1) % 3, (r + 2) % 3
        arrived(phase2[r])
        sum2_ref[r] = (sum1_ref[r, span(coord[b], piece), :] + got2_ref[r, 0]) + (got2_ref[r, 1] + got2_ref[r, 2])
        phase3.append([
            remote(sum2_ref.at[r], got3_ref.at[r, k - 1], s3.at[r, k - 1], r3.at[r, k - 1], peer_of(where, d, k))
            for k in hops])
    phase4 = []
    for r in range(3):
        b = (r + 1) % 3
        arrived(phase3[r])
        mine = span(coord[r] * 4 + coord[b], piece)
        sums_ref[r, mine, :] = (sum2_ref[r] + got3_ref[r, 0]) + (got3_ref[r, 1] + got3_ref[r, 2])
        own = sums_ref.at[r, mine]
        phase4.append([remote(own, own, s4.at[r, k - 1], r4.at[r, k - 1], peer_of(where, b, k)) for k in hops])
    phase5 = []
    for r in range(3):
        arrived(phase4[r])
        own = sums_ref.at[r, span(coord[r], quart)]
        phase5.append([remote(own, own, s5.at[r, k - 1], r5.at[r, k - 1], peer_of(where, r, k)) for k in hops])

    G, M1, T, G2, M2 = range(5)
    partner = peer_of(where, 3, 1)
    final = 5

    def tile(which, part, row, col):
        rows_at = pl.ds(pl.multiple_of(row * BLOCK, BLOCK), BLOCK)
        if which == final:
            return final_ref.at[part, col, rows_at, :]
        return mats_ref.at[which, part, col, rows_at, :]

    def store(which, row, col, value, mirrored):
        values = list(split(value))
        tiles = [tile(which, 0, row, col), tile(which, 1, row, col)]
        if mirrored:
            values += list(split(value.T))
            tiles += [tile(which, 0, col, row), tile(which, 1, col, row)]
        for at, block in zip(tiles, values):
            at[...] = block
        for at in tiles:
            pltpu.make_async_remote_copy(
                src_ref=at, dst_ref=at, send_sem=ps.at[which], recv_sem=pr.at[which],
                device_id=partner, device_id_type=MESH).start()

    def finished(which):
        one = final_ref.at[0] if which == final else mats_ref.at[which, 0]
        pltpu.make_async_copy(one, one, pr.at[which]).wait()

    def diagonal(t):
        slot = 2 * core + t
        return slot, slot

    def beside(t):
        return pair_of(4 + 3 * core + t)

    def block(r, at):
        return sums_ref[r, at * small : (at + 1) * small, :]

    def square(parts4):
        top = jnp.concatenate(parts4[:2], axis=1)
        return jnp.concatenate([top, jnp.concatenate(parts4[2:], axis=1)], axis=0)

    arrived(phase5[0])
    r_at = lax.broadcasted_iota(jnp.int32, (small, small), 0)
    c_at = lax.broadcasted_iota(jnp.int32, (small, small), 1)
    squares = jnp.where(r_at == c_at, (block(0, 0) + block(0, 2)) + (block(0, 3) + block(0, 5)), 0.0)
    squares = jnp.sum(jnp.sum(squares, axis=1, keepdims=True), axis=0, keepdims=True)
    trace_ref[0] = jnp.broadcast_to(squares, trace_ref.shape[1:])
    traced = remote(trace_ref.at[0], trace_ref.at[1], ts, tr, partner)
    for t in range(2):
        value = square([block(0, 3 * t), block(0, 3 * t + 1), block(0, 3 * t + 1).T, block(0, 3 * t + 2)])
        store(G, *diagonal(t), value, False)
    arrived(phase5[1])
    store(G, *beside(0), square([block(1, at) for at in range(4)]), True)
    arrived(phase5[2])
    store(G, *beside(1), square([block(1, 4), block(1, 5), block(2, 4), block(2, 5)]), True)
    store(G, *beside(2), square([block(2, at) for at in range(4)]), True)
    arrived([traced])
    inverse = 1.0 / (jnp.sqrt(trace_ref[0, 0:1, 0:1] + trace_ref[1, 0:1, 0:1]) + EPSILON)
    trace_ref[2] = jnp.broadcast_to(inverse, trace_ref.shape[1:])
    scale_ref[...] = scale_ref[...] * (math.sqrt(OUT) * inverse)
    finished(G)

    def eye(row, col):
        i = lax.broadcasted_iota(jnp.int32, (BLOCK, BLOCK), 0)
        j = lax.broadcasted_iota(jnp.int32, (BLOCK, BLOCK), 1)
        return jnp.where((i == j) & (row == col), 1.0, 0.0)

    def product(left, right, row, col):
        total_block = None
        for k in range(NBLK):
            lh, ll = tile(left, 0, row, k)[...], tile(left, 1, row, k)[...]
            rh, rl = tile(right, 0, k, col)[...], tile(right, 1, k, col)[...]
            term = mxu(lh, rh) + mxu(lh, rl) + mxu(ll, rh)
            total_block = term if total_block is None else total_block + term
        return total_block

    def stage(left, right, dest, finish):
        def off(t, carry):
            row, col = beside(t)
            store(dest, row, col, finish(row, col, product(left, right, row, col)), True)
            return carry

        def on(t, carry):
            row, col = diagonal(t)
            store(dest, row, col, finish(row, col, product(left, right, row, col)), False)
            return carry

        lax.fori_loop(0, 3, off, 0)
        lax.fori_loop(0, 2, on, 0)
        finished(dest)

    def newton(which, scaled):
        def finish(row, col, value):
            own = tile(which, 0, row, col)[...].astype(F32) + tile(which, 1, row, col)[...].astype(F32)
            if scaled:
                inv = trace_ref[2, 0:1, 0:1]
                own = (own * inv) * inv
                value = (((value * inv) * inv) * inv) * inv
            return NEWTON_A * eye(row, col) + NEWTON_B * own + NEWTON_C * value

        return finish

    def normal(row, col, value):
        inv = trace_ref[2, 0:1, 0:1]
        return (value * inv) * inv

    plain = lambda row, col, value: value
    stage(G, G, M1, newton(G, True))
    stage(G, M1, T, normal)
    stage(T, M1, G2, plain)
    stage(G2, G2, M2, newton(G2, False))
    stage(M2, M1, final, plain)
    for copy in started:
        copy.wait_send()
    for which in range(6):
        one = mats_ref.at[0, 0]
        pltpu.make_async_copy(one, one, ps.at[which]).wait()
    for q in range(parts):
        sent = cols_refs[q].at[pl.ds(0, total - 1)]
        pltpu.make_async_copy(sent, sent, gs.at[q]).wait()
        stores[q].wait()


def gather(grads, lat, ids, offsets, scales, momentum):
    rows, latent = lat.shape
    width, count = momentum.shape
    total = grads.shape[1] // count
    parts = len(WIDTHS)
    tasks = rows * total
    size = PACKED // 3
    dma = pltpu.SemaphoreType.DMA
    smem = pl.BlockSpec(memory_space=pltpu.SMEM)
    vmem = pl.BlockSpec(memory_space=pltpu.VMEM)
    anywhere = pl.BlockSpec(memory_space=pl.ANY)
    return pl.pallas_call(
        gather_kernel,
        in_specs=[anywhere, vmem, smem, smem, smem, anywhere],
        out_specs=[vmem, anywhere, vmem],
        out_shape=[
            jax.ShapeDtypeStruct((2, NBLK, width, BLOCK), BF16),
            jax.ShapeDtypeStruct((width, count), F32),
            jax.ShapeDtypeStruct((count // 128, 128), F32),
        ],
        scratch_shapes=[
            pltpu.VMEM((rows, latent + 128), BF16),
            [pltpu.VMEM((total, rows, wide), BF16) for wide in WIDTHS],
            pltpu.VMEM((4, 4, 4, 2, rows, latent + 128), BF16),
            pltpu.VMEM((width, tasks), BF16),
            pltpu.VMEM((width, count), F32),
            pltpu.VMEM((width, count), F32),
            pltpu.VMEM((width, max(WIDTHS)), BF16),
            pltpu.VMEM((width, max(WIDTHS)), BF16),
            pltpu.VMEM((NPAIR, BLOCK, BLOCK), F32),
            pltpu.VMEM((3, size, 128), F32),
            pltpu.VMEM((3, size // 2, 128), F32),
            pltpu.VMEM((3, size // 2, 128), F32),
            pltpu.VMEM((3, 3, size // 8, 128), F32),
            pltpu.VMEM((3, size // 8, 128), F32),
            pltpu.VMEM((3, 3, size // 32, 128), F32),
            pltpu.VMEM((3, size // 32, 128), F32),
            pltpu.VMEM((3, 3, size // 32, 128), F32),
            pltpu.VMEM((3, size // 2, 128), F32),
            pltpu.VMEM((5, 2, NBLK, width, BLOCK), BF16),
            pltpu.VMEM((3, 8, 128), F32),
            dma((parts,)), dma((parts,)), dma, dma((parts,)), dma((parts,)),
        ]
        + [dma((3, 3))] * 6 + [dma, dma, dma((3,)), dma((3,))]
        + [dma((3, 3))] * 10 + [dma, dma, dma((6,)), dma((6,))],
        compiler_params=pltpu.CompilerParams(collective_id=1, has_side_effects=True, vmem_limit_bytes=62 << 20),
        name="gather",
    )(grads, lat, ids, offsets, scales, momentum)


def back_kernel(final_ref, head_ref, mom_ref, scale_ref, newmom_ref, step_ref, high_ref, low_ref):
    new_momentum = MOMENTUM_DECAY * mom_ref[...] + head_ref[...]
    newmom_ref[...] = new_momentum
    high_ref[...], low_ref[...] = split(head_ref[...] + MOMENTUM_DECAY * new_momentum)
    width = CHUNK // 128
    for i in range(NBLK):
        rows = slice(i * BLOCK, (i + 1) * BLOCK)
        total = None
        for k in range(NBLK):
            ks = slice(k * BLOCK, (k + 1) * BLOCK)
            mh, ml = final_ref[0, k, rows, :], final_ref[1, k, rows, :]
            term = mxu(mh, high_ref[ks, :]) + mxu(mh, low_ref[ks, :]) + mxu(ml, high_ref[ks, :])
            total = term if total is None else total + term
        for at in range(width):
            lanes = slice(at * 128, (at + 1) * 128)
            step_ref[rows, lanes] = total[:, lanes] * scale_ref[pl.ds(pl.program_id(0) * width + at, 1), :]


def back(final, head, momentum, scale):
    width, count = head.shape
    return pl.pallas_call(
        back_kernel,
        grid=(count // CHUNK,),
        in_specs=[
            pl.BlockSpec(final.shape, lambda c: (0, 0, 0, 0)),
            pl.BlockSpec((width, CHUNK), lambda c: (0, c)),
            pl.BlockSpec((width, CHUNK), lambda c: (0, c)),
            pl.BlockSpec(scale.shape, lambda c: (0, 0)),
        ],
        out_specs=[pl.BlockSpec((width, CHUNK), lambda c: (0, c))] * 2,
        out_shape=[jax.ShapeDtypeStruct((width, count), F32)] * 2,
        scratch_shapes=[pltpu.VMEM((width, CHUNK), BF16), pltpu.VMEM((width, CHUNK), BF16)],
        compiler_params=pltpu.CompilerParams(vmem_limit_bytes=60 << 20),
        name="back",
    )(final, head, momentum, scale)


def per_device(factor_grads, latents, task_ids, offsets, target_scale, momentum):
    final, head, column_scale = gather(factor_grads, latents, task_ids, offsets, target_scale, momentum)
    new_momentum, step = back(final, head, momentum, column_scale)
    return new_momentum, step


def solution(mesh):
    placed = (
        P(("gx", "gy"), None),
        P(("gx", "gy"), None),
        P(("gx", "gy")),
        P(),
        P(),
        P(None, ("gx", "gy")),
    )
    return jax.shard_map(
        per_device,
        mesh=mesh,
        in_specs=placed,
        out_specs=(P(None, ("gx", "gy")), P(None, ("gx", "gy"))),
        check_vma=False,
    )
```

```python
import math

import jax
import jax.numpy as jnp
from jax import lax
from jax.experimental import pallas as pl
from jax.experimental.pallas import tpu as pltpu
from jax.sharding import PartitionSpec as P

OUT = 196608
MOMENTUM_DECAY = 0.95
EPSILON = 1e-07
NEWTON_A = 3.4445
NEWTON_B = -4.775
NEWTON_C = 2.0315

BLOCK = 256
NBLK = 4
NPAIR = 10
CHUNK = 512
WIDTHS = (512, 512, 512)
PACKED = 36 * 128
F32 = jnp.float32
BF16 = jnp.bfloat16
MESH = pl.DeviceIdType.MESH


def place():
    gx = lax.axis_index("gx")
    gy = lax.axis_index("gy")
    return lax.div(gx, 4), lax.rem(gx, 4), lax.div(gy, 2), lax.rem(gy, 2)


def peer_of(where, axis, hop):
    x, z, y, core = where
    if axis == 0:
        x = lax.rem(x + hop, 4)
    elif axis == 1:
        y = lax.rem(y + hop, 4)
    elif axis == 2:
        z = lax.rem(z + hop, 4)
    else:
        core = 1 - core
    return (x * 4 + z, y * 2 + core)


def split(value):
    high = value.astype(BF16)
    return high, (value - high.astype(F32)).astype(BF16)


def mxu(left, right):
    return lax.dot_general(left, right, (((1,), (0,)), ((), ())), preferred_element_type=F32)


def mxu_t(left, right):
    return lax.dot_general(left, right, (((1,), (1,)), ((), ())), preferred_element_type=F32)


def pair_of(slot):
    side = lax.div(slot - NBLK, 3)
    turn = slot - NBLK - 3 * side
    row = 2 * side + lax.div(turn, 2)
    col = jnp.where(turn == 0, 2 * side + 1, jnp.where(turn == 1, 2 - side, 3 - 3 * side))
    return jnp.where(slot < NBLK, slot, row), jnp.where(slot < NBLK, slot, col)


def gather_kernel(grads_ref, lat_ref, ids_ref, offsets_ref, scales_ref, mom_ref,
                  final_ref, head_ref, scale_ref,
                  own_ref, cols_refs, lats_ref, tlt_ref, moms_ref, heads_ref, high_ref, low_ref, acc_ref,
                  packed_ref, core_ref, half_ref, got1_ref, sum1_ref, got2_ref, sum2_ref, got3_ref,
                  sums_ref, mats_ref, trace_ref,
                  gs, gr, own_sem, ms, hs, a1, b1, a2, b2, a3, b3, a4, b4,
                  cs, cr, s1, r1, s2, r2, s3, r3, s4, r4, s5, r5, ts, tr, ps, pr):
    where = place()
    x, z, y, core = where
    coord = (x, y, z)
    parts = len(cols_refs)
    total, rows = cols_refs[0].shape[:2]
    widths = [ref.shape[2] for ref in cols_refs]
    begin = [sum(widths[:q]) for q in range(parts)]
    count = sum(widths)
    width = lat_ref.shape[1]
    tasks = total * rows
    me = lax.axis_index("gx") * 8 + lax.axis_index("gy")
    barrier = pltpu.get_barrier_semaphore()
    hops = (2, 1, 3)

    def device(to):
        return (lax.div(to, 8), lax.rem(to, 8))

    def greet(k, carry):
        to = lax.rem(me + lax.rem(k * 37, total), total)
        pl.semaphore_signal(barrier, inc=1, device_id=device(to), device_id_type=MESH)
        return carry

    lax.fori_loop(1, total, greet, 0)

    loads = []
    for q in range(parts):
        lanes = slice(begin[q], begin[q] + widths[q])
        load = pltpu.make_async_copy(mom_ref.at[:, lanes], moms_ref.at[:, lanes], ms.at[q])
        load.start()
        loads.append(load)

    own_ref[:, :width] = lat_ref[...]
    at_row = lax.broadcasted_iota(jnp.int32, (rows, 128), 0)
    at_lane = lax.broadcasted_iota(jnp.int32, (rows, 128), 1)
    ids = jnp.zeros((rows, 128), jnp.int32)
    for r in range(rows):
        ids = jnp.where(at_row == r, ids_ref[r], ids)
    fine = jnp.bitwise_and(ids, 15)
    tail = jnp.where(at_lane == 0, ids - fine, jnp.where(at_lane == 1, fine, 0))
    own_ref[:, width:] = tail.astype(F32).astype(BF16)

    column = me * count + 128 * lax.broadcasted_iota(jnp.int32, scale_ref.shape, 0)
    column = column + lax.broadcasted_iota(jnp.int32, scale_ref.shape, 1)

    def level(t, value):
        return jnp.where(column >= offsets_ref[t], scales_ref[t], value)

    scale_ref[...] = lax.fori_loop(0, offsets_ref.shape[0], level, jnp.zeros(scale_ref.shape, F32))

    pl.semaphore_wait(barrier, total - 1)

    started = []

    def remote(src, dst, ssem, rsem, dev):
        copy = pltpu.make_async_remote_copy(
            src_ref=src, dst_ref=dst, send_sem=ssem, recv_sem=rsem, device_id=dev, device_id_type=MESH)
        copy.start()
        started.append(copy)
        return copy

    def arrived(copies):
        for copy in copies:
            copy.wait_recv()

    keep = pltpu.make_async_copy(own_ref, lats_ref.at[x, z, y, core], own_sem)
    keep.start()
    third = (width + 128) // 3
    orders = ((1, 2, 0), (2, 0, 1), (0, 1, 2))

    def region(p, level):
        full = orders[p][:level]
        at = tuple(slice(None) if axis in full else coord[axis] for axis in (0, 2, 1))
        return lats_ref.at[at + (core, slice(None), slice(p * third, (p + 1) * third))]

    def spread(level, ssem, rsem):
        copies = []
        for p in range(3):
            source = own_ref.at[:, p * third : (p + 1) * third] if level == 0 else region(p, level)
            for k in hops:
                copies.append(remote(source, region(p, level), ssem.at[p, k - 1], rsem.at[p, k - 1],
                                     peer_of(where, orders[p][level], k)))
        return copies

    first = spread(0, a1, b1)

    def columns_of(owner, q):
        return grads_ref.at[:, pl.ds(pl.multiple_of(owner * count + begin[q], 128), widths[q])]

    for q in range(parts):
        pltpu.make_async_copy(columns_of(me, q), cols_refs[q].at[me], gr.at[q]).start()

    def send(q, low, high):
        def body(k, carry):
            to = lax.rem(me + lax.rem(k * 37, total), total)
            pltpu.make_async_remote_copy(
                src_ref=columns_of(to, q), dst_ref=cols_refs[q].at[me], send_sem=gs.at[q], recv_sem=gr.at[q],
                device_id=device(to), device_id_type=MESH).start()
            return carry

        lax.fori_loop(low, high, body, 0)

    send(0, 1, 48)
    keep.wait()
    arrived(first)
    second = spread(1, a2, b2)
    send(0, 48, 88)
    arrived(second)
    rest = spread(2, a3, b3)
    send(0, 88, total)
    for q in range(1, parts):
        send(q, 1, total)
    arrived(rest)
    part = lats_ref.at[:, :, :, core]
    arrived([remote(part, part, a4, b4, peer_of(where, 3, 1))])

    def flat(value):
        value = value.astype(F32).reshape(total // 2, 2, rows, value.shape[-1])
        return jnp.concatenate([value[:, 0], value[:, 1]], axis=1).reshape(tasks, value.shape[-1])

    lat = flat(lats_ref[...].reshape(total, rows, width + 128))
    task = jnp.sum(lat[:, width:], axis=1, keepdims=True)
    which = lax.broadcasted_iota(jnp.int32, (tasks, tasks), 1).astype(F32)
    onehot = jnp.where(which == task, 1.0, 0.0).astype(BF16)
    tlt_ref[...] = mxu(onehot, lat[:, :width].astype(BF16)).T.astype(BF16)
    acc_ref[...] = jnp.zeros_like(acc_ref)

    def gram(used, low, high):
        def body(slot, carry):
            row, col = pair_of(slot)
            top = pl.ds(pl.multiple_of(row * BLOCK, BLOCK), BLOCK)
            side = pl.ds(pl.multiple_of(col * BLOCK, BLOCK), BLOCK)
            acc_ref[slot] += (
                mxu_t(high_ref[top, :used], high_ref[side, :used])
                + mxu_t(high_ref[top, :used], low_ref[side, :used])
                + mxu_t(low_ref[top, :used], high_ref[side, :used])
            )
            return carry

        lax.fori_loop(low, high, body, 0)

    def blend(q):
        pltpu.make_async_copy(cols_refs[q], cols_refs[q], gr.at[q]).wait()
        loads[q].wait()
        cols = flat(cols_refs[q][...]).astype(BF16)
        lanes = slice(begin[q], begin[q] + widths[q])
        for i in range(NBLK):
            at = slice(i * BLOCK, (i + 1) * BLOCK)
            head = mxu(tlt_ref[at, :], cols)
            heads_ref[at, lanes] = head
            new_momentum = MOMENTUM_DECAY * moms_ref[at, lanes] + head
            high, low = split(head + MOMENTUM_DECAY * new_momentum)
            high_ref[at, : widths[q]] = high
            low_ref[at, : widths[q]] = low
        store = pltpu.make_async_copy(heads_ref.at[:, lanes], head_ref.at[:, lanes], hs.at[q])
        store.start()
        return store

    stores = []
    for q in range(parts - 1):
        stores.append(blend(q))
        gram(widths[q], 0, NPAIR)
    stores.append(blend(parts - 1))

    other = 1 - core
    size = packed_ref.shape[1]
    halfs, quart, piece = size // 2, size // 8, size // 32
    small = BLOCK // 2

    def span(index, length):
        return pl.ds(pl.multiple_of(index * length, 8), length)

    cored = []
    groups = (((0, 4),), ((4, 6), (7, 9)), ((6, 7), (9, 10)))
    every = tuple((i, j) for i in range(2) for j in range(2))
    layout = (
        tuple((slot, q) for slot in range(NBLK) for q in ((0, 0), (0, 1), (1, 1))),
        tuple((4, q) for q in every) + tuple((5, q) for q in every[:2])
        + tuple((7, q) for q in every) + tuple((8, q) for q in every[:2]),
        tuple((6, q) for q in every) + tuple((5, q) for q in every[2:])
        + tuple((9, q) for q in every) + tuple((8, q) for q in every[2:]),
    )
    phase = []

    def scatter(r):
        cored[r].wait_recv()
        half_ref[r] = packed_ref[r, span(core, halfs), :] + core_ref[r]
        phase.append([
            remote(half_ref.at[r, span(lax.rem(coord[r] + k, 4), quart)], got1_ref.at[r, k - 1],
                   s1.at[r, k - 1], r1.at[r, k - 1], peer_of(where, r, k)) for k in hops])

    for r in range(3):
        for low, high in groups[r]:
            gram(widths[-1], low, high)
        for at, (slot, (i, j)) in enumerate(layout[r]):
            packed_ref[r, at * small : (at + 1) * small, :] = acc_ref[slot, i * small : (i + 1) * small, j * small : (j + 1) * small]
        cored.append(remote(packed_ref.at[r, span(other, halfs)], core_ref.at[r], cs.at[r], cr.at[r], peer_of(where, 3, 1)))
        if r:
            scatter(r - 1)
    scatter(2)
    phase2 = []
    for r in range(3):
        b = (r + 1) % 3
        arrived(phase[r])
        sum1_ref[r] = (half_ref[r, span(coord[r], quart), :] + got1_ref[r, 0]) + (got1_ref[r, 1] + got1_ref[r, 2])
        phase2.append([
            remote(sum1_ref.at[r, span(lax.rem(coord[b] + k, 4), piece)], got2_ref.at[r, k - 1],
                   s2.at[r, k - 1], r2.at[r, k - 1], peer_of(where, b, k)) for k in hops])
    phase3 = []
    for r in range(3):
        b, d = (r + 1) % 3, (r + 2) % 3
        arrived(phase2[r])
        sum2_ref[r] = (sum1_ref[r, span(coord[b], piece), :] + got2_ref[r, 0]) + (got2_ref[r, 1] + got2_ref[r, 2])
        phase3.append([
            remote(sum2_ref.at[r], got3_ref.at[r, k - 1], s3.at[r, k - 1], r3.at[r, k - 1], peer_of(where, d, k))
            for k in hops])
    phase4 = []
    for r in range(3):
        b = (r + 1) % 3
        arrived(phase3[r])
        mine = span(coord[r] * 4 + coord[b], piece)
        sums_ref[r, mine, :] = (sum2_ref[r] + got3_ref[r, 0]) + (got3_ref[r, 1] + got3_ref[r, 2])
        own = sums_ref.at[r, mine]
        phase4.append([remote(own, own, s4.at[r, k - 1], r4.at[r, k - 1], peer_of(where, b, k)) for k in hops])
    phase5 = []
    for r in range(3):
        arrived(phase4[r])
        own = sums_ref.at[r, span(coord[r], quart)]
        phase5.append([remote(own, own, s5.at[r, k - 1], r5.at[r, k - 1], peer_of(where, r, k)) for k in hops])

    G, M1, T, G2, M2 = range(5)
    partner = peer_of(where, 3, 1)
    final = 5

    def tile(which, part, row, col):
        rows_at = pl.ds(pl.multiple_of(row * BLOCK, BLOCK), BLOCK)
        if which == final:
            return final_ref.at[part, col, rows_at, :]
        return mats_ref.at[which, part, col, rows_at, :]

    mine_a, mine_b = 2 * core, 2 * core + 1
    far_e, far_f = 2 - core, 3 - 3 * core
    corner_a, corner_b = (mine_a, mine_a), (mine_b, mine_b)
    joint, cross_a, cross_b = (mine_a, mine_b), (mine_a, far_e), (mine_b, far_f)

    def put(which, row, col, value):
        for part, half_value in enumerate(split(value)):
            tile(which, part, row, col)[...] = half_value

    def push(which, *spots):
        for row, col in spots:
            for part in range(2):
                at = tile(which, part, row, col)
                pltpu.make_async_remote_copy(
                    src_ref=at, dst_ref=at, send_sem=ps.at[which], recv_sem=pr.at[which],
                    device_id=partner, device_id_type=MESH).start()

    def store(which, spot, value):
        row, col = spot
        put(which, row, col, value)
        if spot is corner_a or spot is corner_b:
            return lambda: push(which, spot)
        put(which, col, row, value.T)
        if which == final:
            return lambda: push(which, spot, (col, row))
        if spot is joint:
            return lambda: push(which, (1 + core, 3 * core))
        return lambda: push(which, (col, row))

    def tiles_of(which):
        return mats_ref.at[0, 0] if which == final else mats_ref.at[0, 0, :, : 5 * BLOCK // 2, :]

    def finished(which):
        one = tiles_of(which)
        pltpu.make_async_copy(one, one, pr.at[which]).wait()

    def block(r, at):
        return sums_ref[r, at * small : (at + 1) * small, :]

    def square(parts4):
        top = jnp.concatenate(parts4[:2], axis=1)
        return jnp.concatenate([top, jnp.concatenate(parts4[2:], axis=1)], axis=0)

    arrived(phase5[0])
    r_at = lax.broadcasted_iota(jnp.int32, (small, small), 0)
    c_at = lax.broadcasted_iota(jnp.int32, (small, small), 1)
    squares = jnp.where(r_at == c_at, (block(0, 0) + block(0, 2)) + (block(0, 3) + block(0, 5)), 0.0)
    squares = jnp.sum(jnp.sum(squares, axis=1, keepdims=True), axis=0, keepdims=True)
    trace_ref[0] = jnp.broadcast_to(squares, trace_ref.shape[1:])
    traced = remote(trace_ref.at[0], trace_ref.at[1], ts, tr, partner)
    for t, spot in enumerate((corner_a, corner_b)):
        store(G, spot, square([block(0, 3 * t), block(0, 3 * t + 1), block(0, 3 * t + 1).T, block(0, 3 * t + 2)]))()
    arrived(phase5[1])
    store(G, joint, square([block(1, at) for at in range(4)]))()
    arrived(phase5[2])
    store(G, cross_a, square([block(1, 4), block(1, 5), block(2, 4), block(2, 5)]))()
    store(G, cross_b, square([block(2, at) for at in range(4)]))()
    arrived([traced])
    inverse = 1.0 / (jnp.sqrt(trace_ref[0, 0:1, 0:1] + trace_ref[1, 0:1, 0:1]) + EPSILON)
    trace_ref[2] = jnp.broadcast_to(inverse, trace_ref.shape[1:])
    scale_ref[...] = scale_ref[...] * (math.sqrt(OUT) * inverse)

    def eye(row, col):
        i = lax.broadcasted_iota(jnp.int32, (BLOCK, BLOCK), 0)
        j = lax.broadcasted_iota(jnp.int32, (BLOCK, BLOCK), 1)
        return jnp.where((i == j) & (row == col), 1.0, 0.0)

    def triple(left, right, at, other_at, flip):
        dot = mxu_t if flip else mxu
        lh, ll = tile(left, 0, *at)[...], tile(left, 1, *at)[...]
        rh, rl = tile(right, 0, *other_at)[...], tile(right, 1, *other_at)[...]
        return dot(lh, rh) + dot(lh, rl) + dot(ll, rh)

    def rows_of(left, right, row, col, ks):
        return sum(triple(left, right, (row, k), (col, k), True) for k in ks)

    def stage(left, right, dest, finish, latest):
        value_a = rows_of(left, right, mine_a, mine_a, (mine_a, mine_b, far_e))
        value_b = rows_of(left, right, mine_b, mine_b, (mine_a, mine_b, far_f))
        value_j = rows_of(left, right, mine_a, mine_b, (mine_a, mine_b))
        finished(latest)
        value_a += rows_of(left, right, mine_a, mine_a, (far_f,))
        value_b += rows_of(left, right, mine_b, mine_b, (far_e,))
        pushes = [store(dest, corner_a, finish(*corner_a, value_a)), store(dest, corner_b, finish(*corner_b, value_b))]
        value_j += rows_of(left, right, mine_a, mine_b, (far_e, far_f))
        for go in pushes:
            go()
        value = sum(triple(left, right, (mine_a, k), (k, far_e), False) for k in (mine_a, mine_b, far_e))
        value += triple(left, right, (mine_a, far_f), (far_e, far_f), True)
        store(dest, joint, finish(*joint, value_j))()
        value_b = sum(triple(left, right, (mine_b, k), (k, far_f), False) for k in (mine_a, mine_b, far_e, far_f))
        store(dest, cross_a, finish(*cross_a, value))()
        store(dest, cross_b, finish(*cross_b, value_b))()

    def newton(which, scaled):
        def finish(row, col, value):
            own = tile(which, 0, row, col)[...].astype(F32) + tile(which, 1, row, col)[...].astype(F32)
            if scaled:
                inv = trace_ref[2, 0:1, 0:1]
                own = (own * inv) * inv
                value = (((value * inv) * inv) * inv) * inv
            return NEWTON_A * eye(row, col) + NEWTON_B * own + NEWTON_C * value

        return finish

    def normal(row, col, value):
        inv = trace_ref[2, 0:1, 0:1]
        return (value * inv) * inv

    plain = lambda row, col, value: value
    stage(G, G, M1, newton(G, True), G)
    stage(G, M1, T, normal, M1)
    stage(T, M1, G2, plain, T)
    stage(G2, G2, M2, newton(G2, False), G2)
    stage(M2, M1, final, plain, M2)
    finished(final)
    for copy in started:
        copy.wait_send()
    for which in range(6):
        one = tiles_of(which)
        pltpu.make_async_copy(one, one, ps.at[which]).wait()
    for q in range(parts):
        sent = cols_refs[q].at[pl.ds(0, total - 1)]
        pltpu.make_async_copy(sent, sent, gs.at[q]).wait()
        stores[q].wait()


def gather(grads, lat, ids, offsets, scales, momentum):
    rows, latent = lat.shape
    width, count = momentum.shape
    total = grads.shape[1] // count
    parts = len(WIDTHS)
    tasks = rows * total
    size = PACKED // 3
    dma = pltpu.SemaphoreType.DMA
    smem = pl.BlockSpec(memory_space=pltpu.SMEM)
    vmem = pl.BlockSpec(memory_space=pltpu.VMEM)
    anywhere = pl.BlockSpec(memory_space=pl.ANY)
    return pl.pallas_call(
        gather_kernel,
        in_specs=[anywhere, vmem, smem, smem, smem, anywhere],
        out_specs=[vmem, anywhere, vmem],
        out_shape=[
            jax.ShapeDtypeStruct((2, NBLK, width, BLOCK), BF16),
            jax.ShapeDtypeStruct((width, count), F32),
            jax.ShapeDtypeStruct((count // 128, 128), F32),
        ],
        scratch_shapes=[
            pltpu.VMEM((rows, latent + 128), BF16),
            [pltpu.VMEM((total, rows, wide), BF16) for wide in WIDTHS],
            pltpu.VMEM((4, 4, 4, 2, rows, latent + 128), BF16),
            pltpu.VMEM((width, tasks), BF16),
            pltpu.VMEM((width, count), F32),
            pltpu.VMEM((width, count), F32),
            pltpu.VMEM((width, max(WIDTHS)), BF16),
            pltpu.VMEM((width, max(WIDTHS)), BF16),
            pltpu.VMEM((NPAIR, BLOCK, BLOCK), F32),
            pltpu.VMEM((3, size, 128), F32),
            pltpu.VMEM((3, size // 2, 128), F32),
            pltpu.VMEM((3, size // 2, 128), F32),
            pltpu.VMEM((3, 3, size // 8, 128), F32),
            pltpu.VMEM((3, size // 8, 128), F32),
            pltpu.VMEM((3, 3, size // 32, 128), F32),
            pltpu.VMEM((3, size // 32, 128), F32),
            pltpu.VMEM((3, 3, size // 32, 128), F32),
            pltpu.VMEM((3, size // 2, 128), F32),
            pltpu.VMEM((5, 2, NBLK, width, BLOCK), BF16),
            pltpu.VMEM((3, 8, 128), F32),
            dma((parts,)), dma((parts,)), dma, dma((parts,)), dma((parts,)),
        ]
        + [dma((3, 3))] * 6 + [dma, dma, dma((3,)), dma((3,))]
        + [dma((3, 3))] * 10 + [dma, dma, dma((6,)), dma((6,))],
        compiler_params=pltpu.CompilerParams(collective_id=1, has_side_effects=True, vmem_limit_bytes=62 << 20),
        name="gather",
    )(grads, lat, ids, offsets, scales, momentum)


def back_kernel(final_ref, head_ref, mom_ref, scale_ref, newmom_ref, step_ref, high_ref, low_ref):
    new_momentum = MOMENTUM_DECAY * mom_ref[...] + head_ref[...]
    newmom_ref[...] = new_momentum
    high_ref[...], low_ref[...] = split(head_ref[...] + MOMENTUM_DECAY * new_momentum)
    width = CHUNK // 128
    for i in range(NBLK):
        rows = slice(i * BLOCK, (i + 1) * BLOCK)
        total = None
        for k in range(NBLK):
            ks = slice(k * BLOCK, (k + 1) * BLOCK)
            mh, ml = final_ref[0, k, rows, :], final_ref[1, k, rows, :]
            term = mxu(mh, high_ref[ks, :]) + mxu(mh, low_ref[ks, :]) + mxu(ml, high_ref[ks, :])
            total = term if total is None else total + term
        for at in range(width):
            lanes = slice(at * 128, (at + 1) * 128)
            step_ref[rows, lanes] = total[:, lanes] * scale_ref[pl.ds(pl.program_id(0) * width + at, 1), :]


def back(final, head, momentum, scale):
    width, count = head.shape
    return pl.pallas_call(
        back_kernel,
        grid=(count // CHUNK,),
        in_specs=[
            pl.BlockSpec(final.shape, lambda c: (0, 0, 0, 0)),
            pl.BlockSpec((width, CHUNK), lambda c: (0, c)),
            pl.BlockSpec((width, CHUNK), lambda c: (0, c)),
            pl.BlockSpec(scale.shape, lambda c: (0, 0)),
        ],
        out_specs=[pl.BlockSpec((width, CHUNK), lambda c: (0, c))] * 2,
        out_shape=[jax.ShapeDtypeStruct((width, count), F32)] * 2,
        scratch_shapes=[pltpu.VMEM((width, CHUNK), BF16), pltpu.VMEM((width, CHUNK), BF16)],
        compiler_params=pltpu.CompilerParams(vmem_limit_bytes=60 << 20),
        name="back",
    )(final, head, momentum, scale)


def per_device(factor_grads, latents, task_ids, offsets, target_scale, momentum):
    final, head, column_scale = gather(factor_grads, latents, task_ids, offsets, target_scale, momentum)
    new_momentum, step = back(final, head, momentum, column_scale)
    return new_momentum, step


def solution(mesh):
    placed = (
        P(("gx", "gy"), None),
        P(("gx", "gy"), None),
        P(("gx", "gy")),
        P(),
        P(),
        P(None, ("gx", "gy")),
    )
    return jax.shard_map(
        per_device,
        mesh=mesh,
        in_specs=placed,
        out_specs=(P(None, ("gx", "gy")), P(None, ("gx", "gy"))),
        check_vma=False,
    )
```

```python
import math

import jax
import jax.numpy as jnp
from jax import lax
from jax.experimental import pallas as pl
from jax.experimental.pallas import tpu as pltpu
from jax.sharding import PartitionSpec as P

OUT = 196608
MOMENTUM_DECAY = 0.95
EPSILON = 1e-07
NEWTON_A = 3.4445
NEWTON_B = -4.775
NEWTON_C = 2.0315

BLOCK = 256
NBLK = 4
NPAIR = 10
CHUNK = 512
WIDTHS = (512, 512, 512)
PACKED = 36 * 128
F32 = jnp.float32
BF16 = jnp.bfloat16
MESH = pl.DeviceIdType.MESH


def place():
    gx = lax.axis_index("gx")
    gy = lax.axis_index("gy")
    return lax.div(gx, 4), lax.rem(gx, 4), lax.div(gy, 2), lax.rem(gy, 2)


def peer_of(where, axis, hop):
    x, z, y, core = where
    if axis == 0:
        x = lax.rem(x + hop, 4)
    elif axis == 1:
        y = lax.rem(y + hop, 4)
    elif axis == 2:
        z = lax.rem(z + hop, 4)
    else:
        core = 1 - core
    return (x * 4 + z, y * 2 + core)


def split(value):
    high = value.astype(BF16)
    return high, (value - high.astype(F32)).astype(BF16)


def mxu(left, right):
    return lax.dot_general(left, right, (((1,), (0,)), ((), ())), preferred_element_type=F32)


def mxu_t(left, right):
    return lax.dot_general(left, right, (((1,), (1,)), ((), ())), preferred_element_type=F32)


def pair_of(slot):
    side = lax.div(slot - NBLK, 3)
    turn = slot - NBLK - 3 * side
    row = 2 * side + lax.div(turn, 2)
    col = jnp.where(turn == 0, 2 * side + 1, jnp.where(turn == 1, 2 - side, 3 - 3 * side))
    return jnp.where(slot < NBLK, slot, row), jnp.where(slot < NBLK, slot, col)


def gather_kernel(grads_ref, lat_ref, ids_ref, offsets_ref, scales_ref, mom_ref,
                  final_ref, head_ref, scale_ref,
                  own_ref, cols_refs, lats_ref, tlt_ref, moms_ref, heads_ref, high_ref, low_ref, acc_ref,
                  packed_ref, core_ref, half_ref, got1_ref, sum1_ref, got2_ref, sum2_ref, got3_ref,
                  sums_ref, mats_ref, trace_ref,
                  gs, gr, own_sem, ms, hs, a1, b1, a2, b2, a3, b3, a4, b4,
                  cs, cr, s1, r1, s2, r2, s3, r3, s4, r4, s5, r5, ts, tr, ps, pr):
    where = place()
    x, z, y, core = where
    coord = (x, y, z)
    parts = len(cols_refs)
    total, rows = cols_refs[0].shape[:2]
    widths = [ref.shape[2] for ref in cols_refs]
    begin = [sum(widths[:q]) for q in range(parts)]
    count = sum(widths)
    width = lat_ref.shape[1]
    tasks = total * rows
    me = lax.axis_index("gx") * 8 + lax.axis_index("gy")
    barrier = pltpu.get_barrier_semaphore()
    hops = (2, 1, 3)

    def device(to):
        return (lax.div(to, 8), lax.rem(to, 8))

    def several(low, high, one):
        groups = (high - low) // 4

        def body(i, carry):
            for j in range(4):
                one(low + 4 * i + j)
            return carry

        lax.fori_loop(0, groups, body, 0)
        for k in range(low + 4 * groups, high):
            one(k)

    def greet(k):
        to = lax.rem(me + k * 37, total)
        pl.semaphore_signal(barrier, inc=1, device_id=device(to), device_id_type=MESH)

    several(1, total, greet)

    loads = []
    for q in range(parts):
        lanes = slice(begin[q], begin[q] + widths[q])
        load = pltpu.make_async_copy(mom_ref.at[:, lanes], moms_ref.at[:, lanes], ms.at[q])
        load.start()
        loads.append(load)

    own_ref[:, :width] = lat_ref[...]
    at_row = lax.broadcasted_iota(jnp.int32, (rows, 128), 0)
    at_lane = lax.broadcasted_iota(jnp.int32, (rows, 128), 1)
    ids = jnp.zeros((rows, 128), jnp.int32)
    for r in range(rows):
        ids = jnp.where(at_row == r, ids_ref[r], ids)
    fine = jnp.bitwise_and(ids, 15)
    tail = jnp.where(at_lane == 0, ids - fine, jnp.where(at_lane == 1, fine, 0))
    own_ref[:, width:] = tail.astype(F32).astype(BF16)

    column = me * count + 128 * lax.broadcasted_iota(jnp.int32, scale_ref.shape, 0)
    column = column + lax.broadcasted_iota(jnp.int32, scale_ref.shape, 1)

    def level(t, value):
        return jnp.where(column >= offsets_ref[t], scales_ref[t], value)

    scale_ref[...] = lax.fori_loop(0, offsets_ref.shape[0], level, jnp.zeros(scale_ref.shape, F32))

    pl.semaphore_wait(barrier, total - 1)

    started = []

    def remote(src, dst, ssem, rsem, dev):
        copy = pltpu.make_async_remote_copy(
            src_ref=src, dst_ref=dst, send_sem=ssem, recv_sem=rsem, device_id=dev, device_id_type=MESH)
        copy.start()
        started.append(copy)
        return copy

    def arrived(copies):
        for copy in copies:
            copy.wait_recv()

    keep = pltpu.make_async_copy(own_ref, lats_ref.at[x, z, y, core], own_sem)
    keep.start()
    third = (width + 128) // 3
    orders = ((1, 2, 0), (2, 0, 1), (0, 1, 2))

    def region(p, level):
        full = orders[p][:level]
        at = tuple(slice(None) if axis in full else coord[axis] for axis in (0, 2, 1))
        return lats_ref.at[at + (core, slice(None), slice(p * third, (p + 1) * third))]

    def spread(level, ssem, rsem):
        copies = []
        for p in range(3):
            source = own_ref.at[:, p * third : (p + 1) * third] if level == 0 else region(p, level)
            for k in hops:
                copies.append(remote(source, region(p, level), ssem.at[p, k - 1], rsem.at[p, k - 1],
                                     peer_of(where, orders[p][level], k)))
        return copies

    first = spread(0, a1, b1)

    def columns_of(owner, q):
        return grads_ref.at[:, pl.ds(pl.multiple_of(owner * count + begin[q], 128), widths[q])]

    for q in range(parts):
        pltpu.make_async_copy(columns_of(me, q), cols_refs[q].at[me], gr.at[q]).start()

    def send(q, low, high):
        def one(k):
            to = lax.rem(me + k * 37, total)
            pltpu.make_async_remote_copy(
                src_ref=columns_of(to, q), dst_ref=cols_refs[q].at[me], send_sem=gs.at[q], recv_sem=gr.at[q],
                device_id=device(to), device_id_type=MESH).start()

        several(low, high, one)

    send(0, 1, 48)
    keep.wait()
    arrived(first)
    second = spread(1, a2, b2)
    send(0, 48, 88)
    arrived(second)
    rest = spread(2, a3, b3)
    send(0, 88, total)
    for q in range(1, parts):
        send(q, 1, total)
    arrived(rest)
    part = lats_ref.at[:, :, :, core]
    arrived([remote(part, part, a4, b4, peer_of(where, 3, 1))])

    def flat(value):
        value = value.astype(F32).reshape(total // 2, 2, rows, value.shape[-1])
        return jnp.concatenate([value[:, 0], value[:, 1]], axis=1).reshape(tasks, value.shape[-1])

    lat = flat(lats_ref[...].reshape(total, rows, width + 128))
    task = jnp.sum(lat[:, width:], axis=1, keepdims=True)
    which = lax.broadcasted_iota(jnp.int32, (tasks, tasks), 1).astype(F32)
    onehot = jnp.where(which == task, 1.0, 0.0).astype(BF16)
    tlt_ref[...] = mxu(onehot, lat[:, :width].astype(BF16)).T.astype(BF16)
    acc_ref[...] = jnp.zeros_like(acc_ref)

    def gram(used, low, high):
        def body(slot, carry):
            row, col = pair_of(slot)
            top = pl.ds(pl.multiple_of(row * BLOCK, BLOCK), BLOCK)
            side = pl.ds(pl.multiple_of(col * BLOCK, BLOCK), BLOCK)
            acc_ref[slot] += (
                mxu_t(high_ref[top, :used], high_ref[side, :used])
                + mxu_t(high_ref[top, :used], low_ref[side, :used])
                + mxu_t(low_ref[top, :used], high_ref[side, :used])
            )
            return carry

        lax.fori_loop(low, high, body, 0)

    def blend(q):
        pltpu.make_async_copy(cols_refs[q], cols_refs[q], gr.at[q]).wait()
        loads[q].wait()
        cols = flat(cols_refs[q][...]).astype(BF16)
        lanes = slice(begin[q], begin[q] + widths[q])
        for i in range(NBLK):
            at = slice(i * BLOCK, (i + 1) * BLOCK)
            head = mxu(tlt_ref[at, :], cols)
            heads_ref[at, lanes] = head
            new_momentum = MOMENTUM_DECAY * moms_ref[at, lanes] + head
            high, low = split(head + MOMENTUM_DECAY * new_momentum)
            high_ref[at, : widths[q]] = high
            low_ref[at, : widths[q]] = low
        store = pltpu.make_async_copy(heads_ref.at[:, lanes], head_ref.at[:, lanes], hs.at[q])
        store.start()
        return store

    stores = []
    for q in range(parts - 1):
        stores.append(blend(q))
        gram(widths[q], 0, NPAIR)
    stores.append(blend(parts - 1))

    other = 1 - core
    size = packed_ref.shape[1]
    halfs, quart, piece = size // 2, size // 8, size // 32
    small = BLOCK // 2

    def span(index, length):
        return pl.ds(pl.multiple_of(index * length, 8), length)

    cored = []
    groups = (((0, 4),), ((4, 6), (7, 9)), ((6, 7), (9, 10)))
    every = tuple((i, j) for i in range(2) for j in range(2))
    layout = (
        tuple((slot, q) for slot in range(NBLK) for q in ((0, 0), (0, 1), (1, 1))),
        tuple((4, q) for q in every) + tuple((5, q) for q in every[:2])
        + tuple((7, q) for q in every) + tuple((8, q) for q in every[:2]),
        tuple((6, q) for q in every) + tuple((5, q) for q in every[2:])
        + tuple((9, q) for q in every) + tuple((8, q) for q in every[2:]),
    )
    phase = []

    def scatter(r):
        cored[r].wait_recv()
        half_ref[r] = packed_ref[r, span(core, halfs), :] + core_ref[r]
        phase.append([
            remote(half_ref.at[r, span(lax.rem(coord[r] + k, 4), quart)], got1_ref.at[r, k - 1],
                   s1.at[r, k - 1], r1.at[r, k - 1], peer_of(where, r, k)) for k in hops])

    for r in range(3):
        for low, high in groups[r]:
            gram(widths[-1], low, high)
        for at, (slot, (i, j)) in enumerate(layout[r]):
            packed_ref[r, at * small : (at + 1) * small, :] = acc_ref[slot, i * small : (i + 1) * small, j * small : (j + 1) * small]
        cored.append(remote(packed_ref.at[r, span(other, halfs)], core_ref.at[r], cs.at[r], cr.at[r], peer_of(where, 3, 1)))
        if r:
            scatter(r - 1)
    scatter(2)
    phase2 = []
    for r in range(3):
        b = (r + 1) % 3
        arrived(phase[r])
        sum1_ref[r] = (half_ref[r, span(coord[r], quart), :] + got1_ref[r, 0]) + (got1_ref[r, 1] + got1_ref[r, 2])
        phase2.append([
            remote(sum1_ref.at[r, span(lax.rem(coord[b] + k, 4), piece)], got2_ref.at[r, k - 1],
                   s2.at[r, k - 1], r2.at[r, k - 1], peer_of(where, b, k)) for k in hops])
    phase3 = []
    for r in range(3):
        b, d = (r + 1) % 3, (r + 2) % 3
        arrived(phase2[r])
        sum2_ref[r] = (sum1_ref[r, span(coord[b], piece), :] + got2_ref[r, 0]) + (got2_ref[r, 1] + got2_ref[r, 2])
        phase3.append([
            remote(sum2_ref.at[r], got3_ref.at[r, k - 1], s3.at[r, k - 1], r3.at[r, k - 1], peer_of(where, d, k))
            for k in hops])
    phase4 = []
    for r in range(3):
        b = (r + 1) % 3
        arrived(phase3[r])
        mine = span(coord[r] * 4 + coord[b], piece)
        sums_ref[r, mine, :] = (sum2_ref[r] + got3_ref[r, 0]) + (got3_ref[r, 1] + got3_ref[r, 2])
        own = sums_ref.at[r, mine]
        phase4.append([remote(own, own, s4.at[r, k - 1], r4.at[r, k - 1], peer_of(where, b, k)) for k in hops])
    phase5 = []
    for r in range(3):
        arrived(phase4[r])
        own = sums_ref.at[r, span(coord[r], quart)]
        phase5.append([remote(own, own, s5.at[r, k - 1], r5.at[r, k - 1], peer_of(where, r, k)) for k in hops])

    G, M1, T, G2, M2 = range(5)
    partner = peer_of(where, 3, 1)
    final = 5

    def tile(which, part, row, col):
        rows_at = pl.ds(pl.multiple_of(row * BLOCK, BLOCK), BLOCK)
        if which == final:
            return final_ref.at[part, col, rows_at, :]
        return mats_ref.at[which, part, col, rows_at, :]

    mine_a, mine_b = 2 * core, 2 * core + 1
    far_e, far_f = 2 - core, 3 - 3 * core
    corner_a, corner_b = (mine_a, mine_a), (mine_b, mine_b)
    joint, cross_a, cross_b = (mine_a, mine_b), (mine_a, far_e), (mine_b, far_f)

    def put(which, row, col, value):
        for part, half_value in enumerate(split(value)):
            tile(which, part, row, col)[...] = half_value

    def push(which, *spots):
        for row, col in spots:
            for part in range(2):
                at = tile(which, part, row, col)
                pltpu.make_async_remote_copy(
                    src_ref=at, dst_ref=at, send_sem=ps.at[which], recv_sem=pr.at[which],
                    device_id=partner, device_id_type=MESH).start()

    def store(which, spot, value):
        row, col = spot
        put(which, row, col, value)
        if spot is corner_a or spot is corner_b:
            return lambda: push(which, spot)
        put(which, col, row, value.T)
        if which == final:
            return lambda: push(which, spot, (col, row))
        if spot is joint:
            return lambda: push(which, (1 + core, 3 * core))
        return lambda: push(which, (col, row))

    def tiles_of(which):
        return mats_ref.at[0, 0] if which == final else mats_ref.at[0, 0, :, : 5 * BLOCK // 2, :]

    def finished(which):
        one = tiles_of(which)
        pltpu.make_async_copy(one, one, pr.at[which]).wait()

    def block(r, at):
        return sums_ref[r, at * small : (at + 1) * small, :]

    def square(parts4):
        top = jnp.concatenate(parts4[:2], axis=1)
        return jnp.concatenate([top, jnp.concatenate(parts4[2:], axis=1)], axis=0)

    arrived(phase5[0])
    r_at = lax.broadcasted_iota(jnp.int32, (small, small), 0)
    c_at = lax.broadcasted_iota(jnp.int32, (small, small), 1)
    squares = jnp.where(r_at == c_at, (block(0, 0) + block(0, 2)) + (block(0, 3) + block(0, 5)), 0.0)
    squares = jnp.sum(jnp.sum(squares, axis=1, keepdims=True), axis=0, keepdims=True)
    trace_ref[0] = jnp.broadcast_to(squares, trace_ref.shape[1:])
    traced = remote(trace_ref.at[0], trace_ref.at[1], ts, tr, partner)
    for t, spot in enumerate((corner_a, corner_b)):
        store(G, spot, square([block(0, 3 * t), block(0, 3 * t + 1), block(0, 3 * t + 1).T, block(0, 3 * t + 2)]))()
    arrived(phase5[1])
    store(G, joint, square([block(1, at) for at in range(4)]))()
    arrived(phase5[2])
    store(G, cross_a, square([block(1, 4), block(1, 5), block(2, 4), block(2, 5)]))()
    store(G, cross_b, square([block(2, at) for at in range(4)]))()
    arrived([traced])
    inverse = 1.0 / (jnp.sqrt(trace_ref[0, 0:1, 0:1] + trace_ref[1, 0:1, 0:1]) + EPSILON)
    trace_ref[2] = jnp.broadcast_to(inverse, trace_ref.shape[1:])
    scale_ref[...] = scale_ref[...] * (math.sqrt(OUT) * inverse)

    def eye(row, col):
        i = lax.broadcasted_iota(jnp.int32, (BLOCK, BLOCK), 0)
        j = lax.broadcasted_iota(jnp.int32, (BLOCK, BLOCK), 1)
        return jnp.where((i == j) & (row == col), 1.0, 0.0)

    def triple(left, right, at, other_at, flip):
        dot = mxu_t if flip else mxu
        lh, ll = tile(left, 0, *at)[...], tile(left, 1, *at)[...]
        rh, rl = tile(right, 0, *other_at)[...], tile(right, 1, *other_at)[...]
        return dot(lh, rh) + dot(lh, rl) + dot(ll, rh)

    def rows_of(left, right, row, col, ks):
        return sum(triple(left, right, (row, k), (col, k), True) for k in ks)

    def stage(left, right, dest, finish, latest):
        value_a = rows_of(left, right, mine_a, mine_a, (mine_a, mine_b, far_e))
        value_b = rows_of(left, right, mine_b, mine_b, (mine_a, mine_b, far_f))
        value_j = rows_of(left, right, mine_a, mine_b, (mine_a, mine_b))
        finished(latest)
        value_a += rows_of(left, right, mine_a, mine_a, (far_f,))
        value_b += rows_of(left, right, mine_b, mine_b, (far_e,))
        pushes = [store(dest, corner_a, finish(*corner_a, value_a)), store(dest, corner_b, finish(*corner_b, value_b))]
        value_j += rows_of(left, right, mine_a, mine_b, (far_e, far_f))
        for go in pushes:
            go()
        value = sum(triple(left, right, (mine_a, k), (k, far_e), False) for k in (mine_a, mine_b, far_e))
        value += triple(left, right, (mine_a, far_f), (far_e, far_f), True)
        store(dest, joint, finish(*joint, value_j))()
        value_b = sum(triple(left, right, (mine_b, k), (k, far_f), False) for k in (mine_a, mine_b, far_e, far_f))
        store(dest, cross_a, finish(*cross_a, value))()
        store(dest, cross_b, finish(*cross_b, value_b))()

    def newton(which, scaled):
        def finish(row, col, value):
            own = tile(which, 0, row, col)[...].astype(F32) + tile(which, 1, row, col)[...].astype(F32)
            if scaled:
                inv = trace_ref[2, 0:1, 0:1]
                own = (own * inv) * inv
                value = (((value * inv) * inv) * inv) * inv
            return NEWTON_A * eye(row, col) + NEWTON_B * own + NEWTON_C * value

        return finish

    def normal(row, col, value):
        inv = trace_ref[2, 0:1, 0:1]
        return (value * inv) * inv

    plain = lambda row, col, value: value
    stage(G, G, M1, newton(G, True), G)
    stage(G, M1, T, normal, M1)
    stage(T, M1, G2, plain, T)
    stage(G2, G2, M2, newton(G2, False), G2)
    stage(M2, M1, final, plain, M2)
    finished(final)
    for copy in started:
        copy.wait_send()
    for which in range(6):
        one = tiles_of(which)
        pltpu.make_async_copy(one, one, ps.at[which]).wait()
    for q in range(parts):
        sent = cols_refs[q].at[pl.ds(0, total - 1)]
        pltpu.make_async_copy(sent, sent, gs.at[q]).wait()
        stores[q].wait()


def gather(grads, lat, ids, offsets, scales, momentum):
    rows, latent = lat.shape
    width, count = momentum.shape
    total = grads.shape[1] // count
    parts = len(WIDTHS)
    tasks = rows * total
    size = PACKED // 3
    dma = pltpu.SemaphoreType.DMA
    smem = pl.BlockSpec(memory_space=pltpu.SMEM)
    vmem = pl.BlockSpec(memory_space=pltpu.VMEM)
    anywhere = pl.BlockSpec(memory_space=pl.ANY)
    return pl.pallas_call(
        gather_kernel,
        in_specs=[anywhere, vmem, smem, smem, smem, anywhere],
        out_specs=[vmem, anywhere, vmem],
        out_shape=[
            pltpu.VMEM((2, NBLK, width, BLOCK), BF16),
            jax.ShapeDtypeStruct((width, count), F32),
            jax.ShapeDtypeStruct((count // 128, 128), F32),
        ],
        scratch_shapes=[
            pltpu.VMEM((rows, latent + 128), BF16),
            [pltpu.VMEM((total, rows, wide), BF16) for wide in WIDTHS],
            pltpu.VMEM((4, 4, 4, 2, rows, latent + 128), BF16),
            pltpu.VMEM((width, tasks), BF16),
            pltpu.VMEM((width, count), F32),
            pltpu.VMEM((width, count), F32),
            pltpu.VMEM((width, max(WIDTHS)), BF16),
            pltpu.VMEM((width, max(WIDTHS)), BF16),
            pltpu.VMEM((NPAIR, BLOCK, BLOCK), F32),
            pltpu.VMEM((3, size, 128), F32),
            pltpu.VMEM((3, size // 2, 128), F32),
            pltpu.VMEM((3, size // 2, 128), F32),
            pltpu.VMEM((3, 3, size // 8, 128), F32),
            pltpu.VMEM((3, size // 8, 128), F32),
            pltpu.VMEM((3, 3, size // 32, 128), F32),
            pltpu.VMEM((3, size // 32, 128), F32),
            pltpu.VMEM((3, 3, size // 32, 128), F32),
            pltpu.VMEM((3, size // 2, 128), F32),
            pltpu.VMEM((5, 2, NBLK, width, BLOCK), BF16),
            pltpu.VMEM((3, 8, 128), F32),
            dma((parts,)), dma((parts,)), dma, dma((parts,)), dma((parts,)),
        ]
        + [dma((3, 3))] * 6 + [dma, dma, dma((3,)), dma((3,))]
        + [dma((3, 3))] * 10 + [dma, dma, dma((6,)), dma((6,))],
        compiler_params=pltpu.CompilerParams(collective_id=1, has_side_effects=True, vmem_limit_bytes=58 << 20),
        name="gather",
    )(grads, lat, ids, offsets, scales, momentum)


def back_kernel(final_ref, head_ref, mom_ref, scale_ref, newmom_ref, step_ref, high_ref, low_ref):
    new_momentum = MOMENTUM_DECAY * mom_ref[...] + head_ref[...]
    newmom_ref[...] = new_momentum
    high_ref[...], low_ref[...] = split(head_ref[...] + MOMENTUM_DECAY * new_momentum)
    width = CHUNK // 128
    for i in range(NBLK):
        rows = slice(i * BLOCK, (i + 1) * BLOCK)
        total = None
        for k in range(NBLK):
            ks = slice(k * BLOCK, (k + 1) * BLOCK)
            mh, ml = final_ref[0, k, rows, :], final_ref[1, k, rows, :]
            term = mxu(mh, high_ref[ks, :]) + mxu(mh, low_ref[ks, :]) + mxu(ml, high_ref[ks, :])
            total = term if total is None else total + term
        for at in range(width):
            lanes = slice(at * 128, (at + 1) * 128)
            step_ref[rows, lanes] = total[:, lanes] * scale_ref[pl.ds(pl.program_id(0) * width + at, 1), :]


def back(final, head, momentum, scale):
    width, count = head.shape
    return pl.pallas_call(
        back_kernel,
        grid=(count // CHUNK,),
        in_specs=[
            pl.BlockSpec(memory_space=pltpu.VMEM),
            pl.BlockSpec((width, CHUNK), lambda c: (0, c)),
            pl.BlockSpec((width, CHUNK), lambda c: (0, c)),
            pl.BlockSpec(scale.shape, lambda c: (0, 0)),
        ],
        out_specs=[pl.BlockSpec((width, CHUNK), lambda c: (0, c))] * 2,
        out_shape=[jax.ShapeDtypeStruct((width, count), F32)] * 2,
        scratch_shapes=[pltpu.VMEM((width, CHUNK), BF16), pltpu.VMEM((width, CHUNK), BF16)],
        compiler_params=pltpu.CompilerParams(vmem_limit_bytes=48 << 20),
        name="back",
    )(final, head, momentum, scale)


def per_device(factor_grads, latents, task_ids, offsets, target_scale, momentum):
    final, head, column_scale = gather(factor_grads, latents, task_ids, offsets, target_scale, momentum)
    new_momentum, step = back(final, head, momentum, column_scale)
    return new_momentum, step


def solution(mesh):
    placed = (
        P(("gx", "gy"), None),
        P(("gx", "gy"), None),
        P(("gx", "gy")),
        P(),
        P(),
        P(None, ("gx", "gy")),
    )
    return jax.shard_map(
        per_device,
        mesh=mesh,
        in_specs=placed,
        out_specs=(P(None, ("gx", "gy")), P(None, ("gx", "gy"))),
        check_vma=False,
    )
```
